32 devices in a mesh: blk: 2 (over x), rows: 16 (over z, y, core).
Axes of the slice: x: 2, y: 2, z: 4, core: 2. Of those that a mesh axis runs over, the one named last changes fastest.
Arguments:
- snapshots: float32 [32768, 512], P('rows', 'blk'), may hold values from -40 to 40
- grades: int32 [512], P('blk'), may hold values from 0 to 7
- mover: int32 [3, 2], P(None, 'blk'), may hold values from 0 to 1
Outputs:
- basis: float32 [32768, 512], P('rows', 'blk')
The draws below stay inside these ranges and needn't reach their ends.
All inputs are finite; a program needn't handle non-finite values.
Results may differ from the reference program's by a relative error of at most 0.0001.
Values sent between devices are 32-bit elements; how exact they have to be, the bound alone decides.
A program may use at most 64 MiB of HBM per device.

```python
import math
import jax
import jax.numpy as jnp
from jax import lax

BW = 128
ROUNDS = 4
NS_STEPS = 3
GRADES = 8
ROWS = 32768
COLS = 512
N_BLK = 2


factor_count = 32


def draw_snapshots(key, part):
    keys = jax.random.split(jax.random.fold_in(key, 11), 4)
    noise = jnp.clip(jax.random.normal(keys[0], (ROWS, COLS), jnp.float32), -6.0, 6.0)
    latent = jnp.clip(jax.random.normal(keys[1], (ROWS, factor_count), jnp.float32), -4.0, 4.0)
    decay = 0.04 * jnp.power(0.9, jnp.arange(factor_count, dtype=jnp.float32))
    loading = jax.random.uniform(keys[2], (factor_count, COLS), jnp.float32, -1.0, 1.0) * decay[:, None]
    common = jnp.dot(latent, loading, precision=jax.lax.Precision.HIGHEST)
    column_scale = jnp.exp(jax.random.uniform(keys[3], (1, COLS), jnp.float32, math.log(0.3), math.log(3.0)))
    values = (noise + common) * column_scale
    return jnp.clip(values, -40.0, 40.0)


def with_ends(entries, rng, least, top_value):
    extent = entries.shape
    index_at = [jax.random.randint(jax.random.fold_in(rng, axis), (), 0, extent[axis]) for axis in range(len(extent))]
    entries = entries.at[tuple(index_at)].set(least)
    longest = extent.index(max(extent))
    index_at[longest] = (index_at[longest] + 1) % extent[longest]
    return entries.at[tuple(index_at)].set(top_value)


def setup_inputs(seed: int = 0) -> dict:
    streams_of = jax.random.split(jax.random.key(seed), 4)
    return {
        "snapshots": draw_snapshots(jax.random.fold_in(streams_of[3], 71), 0),
        "grades": with_ends(jax.random.randint(streams_of[1], (COLS,), 0, GRADES), jax.random.fold_in(streams_of[1], 1), 0, GRADES - 1).astype(jnp.int32),
        "mover": with_ends(jax.random.randint(streams_of[2], (ROUNDS - 1, N_BLK), 0, 2), jax.random.fold_in(streams_of[2], 1), 0, 1).astype(jnp.int32),
    }


epsilon = 1e-06
relaxation = 1.2

def rotation(cross_gram, squares, labels):
    left_scale = lax.rsqrt(squares[:BW] + epsilon)
    right_scale = lax.rsqrt(squares[BW:] + epsilon)
    grade_gap = jnp.abs(labels[:BW, None] - labels[None, BW:])
    scaled = cross_gram * left_scale[:, None] * right_scale[None, :] / (1.0 + grade_gap)
    magnitude = jnp.sqrt(jnp.sum(scaled * scaled) + epsilon)
    generator = relaxation * scaled / magnitude
    zeros_block = jnp.zeros_like(generator)
    upper_half = jnp.concatenate([zeros_block, generator], 1)
    lower_half = jnp.concatenate([-generator.T, zeros_block], 1)
    iterate = jnp.eye(2 * BW, dtype=generator.dtype) + jnp.concatenate([upper_half, lower_half], 0)
    for sweep in range(NS_STEPS):
        product = lax.dot_general(iterate, iterate, (((0,), (0,)), ((), ())), precision=lax.Precision.HIGHEST)
        iterate = 1.5 * iterate - 0.5 * jnp.dot(iterate, product, precision=lax.Precision.HIGHEST)
    return iterate

def reference(snapshots, grades, mover):
    blocks = snapshots.reshape(ROWS, N_BLK, 2 * BW)
    labels = grades.reshape(N_BLK, 2 * BW).astype(snapshots.dtype)
    for round_index in range(ROUNDS):
        cross_gram = jnp.einsum('mpi,mpj->pij', blocks[:, :, :BW], blocks[:, :, BW:], precision=lax.Precision.HIGHEST)
        squares = lax.optimization_barrier(jnp.sum(blocks * blocks, axis=0))
        rotator = jax.vmap(rotation)(cross_gram, squares, labels)
        blocks = jnp.einsum('mpi,pij->mpj', blocks, rotator, precision=lax.Precision.HIGHEST)
        if round_index + 1 < ROUNDS:
            first = mover[round_index] == 0
            first_blocks = first[None, :, None]
            first_labels = first[:, None]
            moving = jnp.where(first_blocks, blocks[:, :, :BW], blocks[:, :, BW:])
            staying = jnp.where(first_blocks, blocks[:, :, BW:], blocks[:, :, :BW])
            move_label = jnp.where(first_labels, labels[:, :BW], labels[:, BW:])
            stay_label = jnp.where(first_labels, labels[:, BW:], labels[:, :BW])
            moving = jnp.roll(moving, 1, axis=1)
            move_label = jnp.roll(move_label, 1, axis=0)
            blocks = jnp.where(first_blocks, jnp.concatenate([moving, staying], 2), jnp.concatenate([staying, moving], 2))
            labels = jnp.where(first_labels, jnp.concatenate([move_label, stay_label], 1), jnp.concatenate([stay_label, move_label], 1))
    return blocks.reshape(ROWS, COLS)
```

```python
import functools

import jax
import jax.numpy as jnp
from jax import lax
from jax.experimental import pallas as pl
from jax.experimental.pallas import tpu as pltpu
from jax.sharding import PartitionSpec as P

BW = 128
ROUNDS = 4
NS_STEPS = 3
CHUNKS = 8
FIRST = 3
SOON = 2
TALL = 2
LOADS = 4
WRITES = 4

epsilon = 1e-06
relaxation = 1.2

MESH = pl.DeviceIdType.MESH
ROWS_DIM = (((0,), (0,)), ((), ()))
PLAIN = (((1,), (0,)), ((), ()))
VMEM = pl.BlockSpec(memory_space=pltpu.VMEM)
ANY = pl.BlockSpec(memory_space=pl.ANY)
HBM = pl.BlockSpec(memory_space=pltpu.HBM)


def from_behind(value, axis, by):
    peers = lax.axis_size(axis)
    return lax.ppermute(value, axis, [(i, (i + by) % peers) for i in range(peers)])


def rotation(cross_gram, squares, labels):
    left_scale = lax.rsqrt(squares[:BW] + epsilon)
    right_scale = lax.rsqrt(squares[BW:] + epsilon)
    grade_gap = jnp.abs(labels[:BW, None] - labels[None, BW:])
    scaled = cross_gram * left_scale[:, None] * right_scale[None, :] / (1.0 + grade_gap)
    magnitude = jnp.sqrt(jnp.sum(scaled * scaled) + epsilon)
    generator = relaxation * scaled / magnitude
    zeros_block = jnp.zeros_like(generator)
    upper_half = jnp.concatenate([zeros_block, generator], 1)
    lower_half = jnp.concatenate([-generator.T, zeros_block], 1)
    iterate = jnp.eye(2 * BW, dtype=generator.dtype) + jnp.concatenate([upper_half, lower_half], 0)
    for sweep in range(NS_STEPS):
        product = lax.dot_general(iterate, iterate, ROWS_DIM, precision=lax.Precision.HIGHEST)
        iterate = 1.5 * iterate - 0.5 * jnp.dot(iterate, product, precision=lax.Precision.HIGHEST)
    return iterate


def statistics(blocks):
    cross_part = lax.dot_general(
        blocks[:, :BW], blocks[:, BW:], ROWS_DIM, precision=lax.Precision.HIGHEST
    )
    square_part = jnp.sum(blocks * blocks, axis=0)
    return lax.psum((cross_part, square_part), "rows")


def assemble(first, incoming, staying):
    return jnp.where(
        first, jnp.concatenate([incoming, staying], -1), jnp.concatenate([staying, incoming], -1)
    )


def general_body(snapshots, grades, mover):
    blocks = snapshots
    labels = grades.astype(jnp.float32)
    for round_index in range(ROUNDS):
        cross_gram, squares = statistics(blocks)
        rotator = rotation(cross_gram, squares, labels)
        blocks = jnp.dot(blocks, rotator, precision=lax.Precision.HIGHEST)
        if round_index + 1 < ROUNDS:
            first = mover[round_index, 0] == 0
            move_label = jnp.where(first, labels[:BW], labels[BW:])
            stay_label = jnp.where(first, labels[BW:], labels[:BW])
            moving = jnp.where(first, blocks[:, :BW], blocks[:, BW:])
            staying = jnp.where(first, blocks[:, BW:], blocks[:, :BW])
            incoming, came_label = from_behind((moving, move_label), "blk", 1)
            blocks = assemble(first, incoming, staying)
            labels = assemble(first, came_label, stay_label)
    return blocks


def split(value):
    high = value.astype(jnp.bfloat16)
    return high, (value - high.astype(jnp.float32)).astype(jnp.bfloat16)


def dot_split(a, b, dims=PLAIN):
    (ah, al), (bh, bl) = a, b
    mul = functools.partial(lax.dot_general, dimension_numbers=dims, preferred_element_type=jnp.float32)
    return mul(ah, bh) + (mul(ah, bl) + mul(al, bh))


def dot3(a, b, dims=PLAIN):
    return dot_split(split(a), split(b), dims)


def dot6(a, b, dims=PLAIN):
    return lax.dot_general(
        a, b, dims, precision=lax.Precision.HIGHEST, preferred_element_type=jnp.float32
    )


def turn_kernel(
    n, x_hbm, grade_hbm, mover_hbm, held_ref,
    x_ref, near_ref, x_high, x_low, near_high, near_low, grade_ref, mover_ref, meta_ref, meta,
    dpart, dgot, dmid, dnear, dall, diag_ref, turn_ref, flip_ref, fac_ref,
    cpart, cgot, cmid, cnear, cmine, cother, cfull,
    high_ref, low_ref,
    x_send, x_recv, rs_send, rs_recv, ag_send, ag_recv, sib_send, sib_recv, one_send, one_recv,
    load_sem, side_sem,
):
    pos, me = lax.axis_index("blk"), lax.axis_index("rows")
    other = 1 - pos
    core, group = lax.rem(me, 2), me // 2
    groups = n // 2
    rows, width = x_ref.shape
    half = rows // 2
    piece = half // CHUNKS
    share = width // n
    partner, sibling = (other, me), (pos, me + 1 - 2 * core)
    peers = [None] + [lax.rem(group + k, groups) for k in range(1, groups)]

    loads = []
    for i in range(LOADS):
        part = pl.ds(i * (rows // LOADS), rows // LOADS)
        loads.append(pltpu.make_async_copy(x_hbm.at[part], x_ref.at[part], load_sem.at[i]))
    sides = [
        pltpu.make_async_copy(grade_hbm, grade_ref, side_sem.at[0]),
        pltpu.make_async_copy(mover_hbm, mover_ref, side_sem.at[1]),
    ]
    for copy in sides + loads:
        copy.start()
    barrier = pltpu.get_barrier_semaphore()
    for device in (partner, sibling):
        pl.semaphore_signal(barrier, inc=1, device_id=device, device_id_type=MESH)
    for peer in peers[1:]:
        pl.semaphore_signal(barrier, inc=1, device_id=(pos, 2 * peer + core), device_id_type=MESH)
    pl.semaphore_wait(barrier, groups + 1)

    def remote(src, dst, send, recv, device):
        copy = pltpu.make_async_remote_copy(
            src_ref=src, dst_ref=dst, send_sem=send, recv_sem=recv,
            device_id=device, device_id_type=MESH,
        )
        copy.start()
        return copy

    def swap(c):
        start = lax.rem(other * half + c * piece, rows)
        source = x_hbm.at[pl.ds(pl.multiple_of(start, piece), piece)]
        return remote(source, near_ref.at[pl.ds(c * piece, piece)], x_send.at[c], x_recv.at[c], partner)

    swaps = [swap(c) for c in range(FIRST)]
    for copy in sides:
        copy.wait()
    meta[...] = jnp.zeros_like(meta)
    meta[0:1, :] = grade_ref[...].astype(jnp.float32)
    for r in range(ROUNDS - 1):
        meta[r + 1:r + 2, :] = jnp.full((1, width), mover_ref[r], jnp.int32).astype(jnp.float32)
    meta_ref[pos] = meta[...]
    labels = remote(meta, meta_ref.at[pos], one_send.at[0], one_recv.at[0], partner)

    def pair_up(part, got, which):
        return remote(part.at[1 - core], got, sib_send.at[which], sib_recv.at[which], sibling)

    def scatter(mid, near, which):
        return [
            remote(
                mid.at[peers[k]], near.at[k], rs_send.at[which, k], rs_recv.at[which, k],
                (pos, 2 * peers[k] + core),
            )
            for k in range(1, groups)
        ]

    def summed(mid, near, copies):
        total = mid[group]
        for k in range(1, groups):
            copies[k - 1].wait()
            total = total + near[k]
        return total

    def gather(full, which):
        return [
            remote(
                full.at[core, group], full.at[core, group], ag_send.at[which, k],
                ag_recv.at[which, k], (pos, 2 * peers[k] + core),
            )
            for k in range(1, groups)
        ]

    def hand_over(full, copies, which):
        for copy in copies:
            copy.wait()
        return remote(full.at[core], full.at[core], sib_send.at[which], sib_recv.at[which], sibling)

    def receive(c):
        swaps[c].wait()
        there = slice(c * piece, (c + 1) * piece)
        near_high[there, :], near_low[there, :] = split(near_ref[there, :])

    def cross(c):
        receive(c)
        here = pl.ds(pl.multiple_of(pos * half + c * piece, piece), piece)
        there = slice(c * piece, (c + 1) * piece)
        mine = x_high[here, :], x_low[here, :]
        theirs = near_high[there, :], near_low[there, :]
        left = [jnp.where(pos == 0, a, b) for a, b in zip(mine, theirs)]
        right = [jnp.where(pos == 0, b, a) for a, b in zip(mine, theirs)]
        return dot_split(left, right, ROWS_DIM)

    both = jnp.zeros((width, 2 * width), jnp.float32)
    for i in range(LOADS):
        loads[i].wait()
        part = slice(i * (rows // LOADS), (i + 1) * (rows // LOADS))
        high, low = split(x_ref[part, :])
        x_high[part, :] = high
        x_low[part, :] = low
        both = both + lax.dot_general(
            high, jnp.concatenate([high, low], 1), ROWS_DIM, preferred_element_type=jnp.float32
        )
    own = both[:, :width] + (both[:, width:] + both[:, width:].T)
    dpart[...] = own.reshape(2, groups, share, width)
    copy = pair_up(dpart, dgot, 0)
    copy.wait()
    dmid[...] = dpart[core] + dgot[...]
    copies = scatter(dmid, dnear, 0)
    total = cross(0)
    dall[pos, core, group] = summed(dmid, dnear, copies)
    mine, theirs = dall.at[pos], dall.at[other]
    here = mine.at[core, group]
    d_swap = remote(here, here, one_send.at[1], one_recv.at[1], partner)
    own_copies = gather(mine, 0)
    swaps += [swap(c) for c in range(FIRST, CHUNKS + SOON)]
    total = total + cross(1)
    d_swap.wait()
    their_copies = gather(theirs, 1)
    own_copy = hand_over(mine, own_copies, 1)
    total = total + cross(2)

    def begin_round(p):
        begin(p, dall[p].reshape(width, width), meta_ref, turn_ref, flip_ref, diag_ref)

    own_copy.wait()
    begin_round(pos)
    their_copy = hand_over(theirs, their_copies, 2)
    total = total + cross(3)
    labels.wait()
    their_copy.wait()
    begin_round(other)
    prepare(pos, meta_ref, diag_ref, fac_ref)
    for c in range(4, CHUNKS):
        total = total + cross(c)
    cpart[...] = total.reshape(2, groups, share, width)
    copy = pair_up(cpart, cgot, 3)
    copy.wait()
    cmid[...] = cpart[core] + cgot[...]
    copies = scatter(cmid, cnear, 1)
    cmine[...] = summed(cmid, cnear, copies)
    c_swap = remote(cmine, cother, one_send.at[2], one_recv.at[2], partner)
    swaps += [swap(c) for c in range(CHUNKS + SOON, 2 * CHUNKS)]
    c_swap.wait()
    cfull[core, group] = cmine[...] + cother[...]
    copies = gather(cfull, 2)
    copy = hand_over(cfull, copies, 4)
    copy.wait()
    chain(
        pos, cfull[...].reshape(width, width), diag_ref, turn_ref, flip_ref, meta_ref, fac_ref,
        high_ref, low_ref,
    )
    tile = TALL * piece
    for t in range(rows // tile):
        for c in range(max(t * TALL, CHUNKS), (t + 1) * TALL):
            receive(c)
        here = pl.ds(pl.multiple_of(lax.rem(pos * half + t * tile, rows), tile), tile)
        there = slice(t * tile, (t + 1) * tile)
        high = jnp.concatenate([x_high[here, :], near_high[there, :]], 1)
        low = jnp.concatenate([x_low[here, :], near_low[there, :]], 1)
        held_ref[here, :] = dot_split((high, low), (high_ref[...], low_ref[...]))


def eye(n):
    return (
        lax.broadcasted_iota(jnp.int32, (n, n), 0) == lax.broadcasted_iota(jnp.int32, (n, n), 1)
    ).astype(jnp.float32)


def cut3(value):
    high, rest = value.astype(jnp.bfloat16), None
    rest = value - high.astype(jnp.float32)
    middle = rest.astype(jnp.bfloat16)
    return high, middle, (rest - middle.astype(jnp.float32)).astype(jnp.bfloat16)


def mul(a, b, dims=PLAIN):
    return lax.dot_general(a, b, dims, preferred_element_type=jnp.float32)


def fine_left(a, b):
    (ah, am, al), (bh, bl) = a, b
    return mul(ah, bh) + ((mul(ah, bl) + mul(am, bh)) + (mul(am, bl) + mul(al, bh)))


def fine_right(a, b):
    (ah, al), (bh, bm, bl) = a, b
    return mul(ah, bh) + ((mul(ah, bm) + mul(al, bh)) + (mul(al, bm) + mul(ah, bl)))


def rotate(crosses, signs, work=()):
    work = list(work)
    unit = eye(BW)
    both = range(2)
    each = range(len(crosses))
    total = [jnp.sum(h * h, keepdims=True) + epsilon for h in crosses]
    cut = [split(h) for h in crosses]
    flip = [split(h.T) for h in crosses]
    scale = [relaxation * relaxation / t for t in total]
    m = [[scale[i] * dot_split(cut[i], flip[i]), scale[i] * dot_split(flip[i], cut[i])] for i in each]
    b = [relaxation * lax.rsqrt(total[i]) * signs[i] * crosses[i] for i in each]
    bc = [split(v) for v in b]
    if work:
        work.pop(0)()
    mc = [[split(v) for v in pair] for pair in m]
    m2 = [[dot_split(v, v) for v in pair] for pair in mc]
    mb = [dot_split(mc[i][0], bc[i]) for i in each]
    if work:
        work.pop(0)()
    m2c = [[split(v) for v in pair] for pair in m2]
    m3 = [[dot_split(m2c[i][j], mc[i][j]) for j in both] for i in each]
    m4 = [[dot_split(v, v) for v in pair] for pair in m2c]
    m2b = [dot_split(m2c[i][0], bc[i]) for i in each]
    m3b = [dot_split(m2c[i][0], split(mb[i])) for i in each]
    if work:
        work.pop(0)()
    n = [[0.75 * m2[i][j] - 0.25 * m3[i][j] for j in both] for i in each]
    p = [
        [
            unit - 0.5 * m[i][j] + 0.375 * m2[i][j] - 0.3125 * m3[i][j] + 0.0625 * m4[i][j]
            for j in both
        ]
        for i in each
    ]
    nb = [split(0.75 * m2b[i] - 0.25 * m3b[i]) for i in each]
    nc = [[split(v) for v in pair] for pair in n]
    pc = [[split(v) for v in pair] for pair in p]
    u = [[split(dot_split(v, v)) for v in pair] for pair in nc]
    r = [[split(dot_split(pc[i][j], split(0.375 * unit + 0.125 * n[i][j]))) for j in both] for i in each]
    pb = [dot_split(pc[i][0], bc[i]) for i in each]
    nnb = [split(dot_split(nc[i][0], nb[i])) for i in each]
    if work:
        work.pop(0)()
    out = []
    for i in each:
        gain = [p[i][j] + dot_split(r[i][j], u[i][j]) for j in both]
        out.append((gain[0], pb[i] + dot_split(r[i][0], nnb[i]), gain[1]))
    for step in work:
        step()
    return out


def columns(q):
    upper, edge, lower = q
    return (
        split(jnp.concatenate([upper, -edge.T], 0)), split(jnp.concatenate([edge, lower], 0))
    )


def turned(q):
    upper, edge, lower = q
    return (
        split(jnp.concatenate([upper, -edge], 1)), split(jnp.concatenate([edge.T, lower], 1))
    )


def choose(flag, a, b):
    return tuple(jnp.where(flag, u, v) for u, v in zip(a, b))


def order(flag, pair):
    return choose(flag, pair[1], pair[0]), choose(flag, pair[0], pair[1])


def beside(a, b, axis=1):
    return tuple(jnp.concatenate([u, v], axis) for u, v in zip(a, b))


def plan(meta_ref):
    flags, signs, kept = [], [], [1.0, 1.0]
    labels = [[meta_ref[p, 0:1, :BW], meta_ref[p, 0:1, BW:]] for p in range(2)]
    names = []
    for r in range(ROUNDS - 1):
        first = [1.0 - meta_ref[p, r + 1:r + 2, :BW] for p in range(2)]
        flag = [jnp.abs(first[p] - kept[p]) < 0.5 for p in range(2)]
        kept = [1.0 - first[0], first[1]]
        labels = [
            [jnp.where(flag[p], labels[p][1], labels[p][0]), jnp.where(flag[p], labels[p][0], labels[p][1])]
            for p in range(2)
        ]
        labels = [[labels[0][0], labels[1][1]], [labels[0][1], labels[1][0]]]
        flags.append(flag)
        signs.append([2.0 * k - 1.0 for k in kept])
        names.append(labels)
    return flags, signs, names


def tall(row):
    return jnp.broadcast_to(row, (BW, BW)).T


def weight(pair):
    return 1.0 / (1.0 + jnp.abs(tall(pair[0]) - pair[1]))


def begin(p, diag, meta_ref, turn_ref, flip_ref, diag_ref):
    unit = eye(BW)
    labels = meta_ref[p, 0:1, :]
    left = jnp.sum(diag[:BW, :BW] * unit, axis=1, keepdims=True)
    right = jnp.sum(diag[BW:, BW:] * unit, axis=0, keepdims=True)
    scale = lax.rsqrt(left + epsilon) * lax.rsqrt(right + epsilon)
    cross = diag[:BW, BW:] * (scale * weight((labels[:, :BW], labels[:, BW:])))
    (q,) = rotate([cross], [1.0])
    flag = meta_ref[p, 1:2, :BW] < 0.5
    q_cut = beside(*order(flag, columns(q)))
    wide = jnp.concatenate([flag, flag], 1)
    flip = beside(*order(wide, turned(q)), 0)
    for k in range(2):
        turn_ref[p, k] = q_cut[k]
        flip_ref[p, k] = flip[k]
    diag_ref[p] = fine_right(flip, cut3(fine_left(cut3(diag), q_cut)))


def prepare(pos, meta_ref, diag_ref, fac_ref):
    unit = eye(BW)
    flags, signs, names = plan(meta_ref)

    def scales(p, s, axis):
        part = slice(s * BW, s * BW + BW)
        return lax.rsqrt(jnp.sum(diag_ref[p, part, part] * unit, axis=axis, keepdims=True) + epsilon)

    fac_ref[0] = weight(names[0][0]) * scales(0, 0, 1) * scales(1, 1, 0)
    fac_ref[1] = weight(names[0][1]) * scales(0, 1, 1) * scales(1, 0, 0)
    fac_ref[2] = weight(names[1][0])
    fac_ref[3] = weight(names[1][1])
    fac_ref[4] = weight([jnp.where(pos == 0, a, b) for a, b in zip(*names[2])])


def chain(pos, cross, diag_ref, turn_ref, flip_ref, meta_ref, fac_ref, high_ref, low_ref):
    assert ROUNDS == 4
    flags, signs, _ = plan(meta_ref)
    low, top = slice(0, BW), slice(BW, 2 * BW)
    turn = [(turn_ref[p, 0], turn_ref[p, 1]) for p in range(2)]
    left = (flip_ref[0, 0], flip_ref[0, 1])

    def part(pair, rows=slice(None), cols=slice(None)):
        return tuple(v[rows, cols] for v in pair)

    held = {}
    mid = cut3(fine_left(cut3(cross), turn[1]))
    x0 = fine_right(part(left, low), part(mid, cols=top))
    x1 = fine_right(part(left, top), part(mid, cols=low))

    def rest():
        held["stay"] = fine_right(part(left, low), part(mid, cols=low))
        held["move"] = fine_right(part(left, top), part(mid, cols=top))

    qs = rotate([x0 * fac_ref[0], x1 * fac_ref[1]], signs[0], [rest])
    d0 = jnp.concatenate([
        jnp.concatenate([diag_ref[0, low, low], x0], 1),
        jnp.concatenate([x0.T, diag_ref[1, top, top]], 1),
    ], 0)
    d1 = jnp.concatenate([
        jnp.concatenate([diag_ref[0, top, top], x1], 1),
        jnp.concatenate([x1.T, diag_ref[1, low, low]], 1),
    ], 0)
    g = jnp.concatenate([
        jnp.concatenate([diag_ref[0, low, top], held["stay"]], 1),
        jnp.concatenate([held["move"].T, diag_ref[1, top, low]], 1),
    ], 0)
    d0, d1, g = cut3(d0), cut3(d1), cut3(g)
    q = [beside(*order(flags[1][p], columns(qs[p]))) for p in range(2)]
    wide = [jnp.concatenate([flags[1][p]] * 2, 1) for p in range(2)]
    qt = [beside(*order(wide[p], turned(qs[p])), 0) for p in range(2)]
    mid = cut3(fine_left(g, q[1]))
    t0 = fine_right(qt[0], d0)
    t1 = fine_left(d1, q[1])
    x0 = fine_right(part(qt[0], low), part(mid, cols=top))
    x1 = fine_right(part(qt[0], top), part(mid, cols=low))

    def full(pair):
        return pair[0].astype(jnp.float32) + pair[1].astype(jnp.float32)

    sq0 = lax.rsqrt(jnp.sum(full(qt[0]) * t0, axis=1, keepdims=True) + epsilon)
    sq1 = lax.rsqrt(jnp.sum(full(q[1]) * t1, axis=0, keepdims=True) + epsilon)

    def rest0():
        held["stay"] = fine_right(part(qt[0], low), part(mid, cols=low))
        held["move"] = fine_right(part(qt[0], top), part(mid, cols=top))
        held["d0"] = fine_left(cut3(t0), q[0])

    def rest1():
        held["d1"] = fine_right(qt[1], cut3(t1))
        held["w00"] = dot_split(part(turn[0], cols=low), part(q[0], low))

    def rest2():
        held["w01"] = dot_split(part(turn[1], cols=top), part(q[0], top))
        held["w10"] = dot_split(part(turn[0], cols=top), part(q[1], low))

    def rest3():
        held["w11"] = dot_split(part(turn[1], cols=low), part(q[1], top))

    qs = rotate(
        [x0 * (fac_ref[2] * sq0[low] * sq1[:, top]), x1 * (fac_ref[3] * sq0[top] * sq1[:, low])],
        signs[1], [rest0, rest1, rest2, rest3],
    )
    e0, e1 = held["d0"], held["d1"]
    d0 = cut3(jnp.concatenate([
        jnp.concatenate([e0[low, low], x0], 1), jnp.concatenate([x0.T, e1[top, top]], 1),
    ], 0))
    d1 = cut3(jnp.concatenate([
        jnp.concatenate([e0[top, top], x1], 1), jnp.concatenate([x1.T, e1[low, low]], 1),
    ], 0))
    g = cut3(jnp.concatenate([
        jnp.concatenate([e0[low, top], held["stay"]], 1),
        jnp.concatenate([held["move"].T, e1[top, low]], 1),
    ], 0))
    mine = pos == 0
    wide = jnp.concatenate([flags[2][0]] * 2, 1)
    stay, move = order(wide, turned(qs[0]))
    up = choose(mine, stay, move)
    stay, move = order(flags[2][0], columns(qs[0]))
    upright = choose(mine, stay, move)
    stay, move = order(flags[2][1], columns(qs[1]))
    side = choose(mine, move, stay)
    mid = cut3(fine_left(g, side))
    t0 = fine_right(up, d0)
    t1 = fine_left(d1, side)
    x = fine_right(up, mid)
    sq0 = lax.rsqrt(jnp.sum(full(up) * t0, axis=1, keepdims=True) + epsilon)
    sq1 = lax.rsqrt(jnp.sum(full(side) * t1, axis=0, keepdims=True) + epsilon)
    rows = [None, None]

    def tail(r):
        def run():
            a, b = held["w0" + str(r)], held["w1" + str(r)]
            first = split(jnp.concatenate([a[:, low], b[:, top]], 1))
            second = split(jnp.concatenate([a[:, top], b[:, low]], 1))
            rows[r] = split(jnp.concatenate([dot_split(first, upright), dot_split(second, side)], 1))
        return run

    sign = jnp.where(mine, signs[2][0], signs[2][1])
    (last,) = rotate([x * (fac_ref[4] * sq0 * sq1)], [sign], [tail(0), tail(1)])
    a, b = columns(last)
    last = beside(choose(sign > 0.0, a, b), choose(sign > 0.0, b, a))
    out = [split(dot_split(rows[r], last)) for r in range(2)]
    width = 2 * BW
    for p in range(2):
        high, lower = choose(mine, out[p], out[1 - p])
        high_ref[p * width:(p + 1) * width] = high
        low_ref[p * width:(p + 1) * width] = lower


def write_kernel(held_ref, out_ref, sems):
    rows = held_ref.shape[0] // WRITES
    copies = []
    for i in range(WRITES):
        part = pl.ds(i * rows, rows)
        copies.append(pltpu.make_async_copy(held_ref.at[part], out_ref.at[part], sems.at[i]))
        copies[-1].start()
    for copy in copies:
        copy.wait()


def pair_body(n, snapshots, grades, mover):
    rows, width = snapshots.shape
    share = width // n
    f32 = jnp.float32
    dma = pltpu.SemaphoreType.DMA
    whole = pltpu.VMEM((2, n // 2, share, width), f32)
    part = pltpu.VMEM((n // 2, share, width), f32)
    one = pltpu.VMEM((share, width), f32)
    everything = pltpu.VMEM((rows, width), f32)
    cut = pltpu.VMEM((rows, width), jnp.bfloat16)
    square = pltpu.VMEM((2, width, width), f32)
    turn = pltpu.VMEM((2, 2, width, width), jnp.bfloat16)
    operands = [
        pltpu.with_memory_space_constraint(value, pltpu.HBM)
        for value in (snapshots, grades.reshape(1, width), mover.reshape(ROUNDS - 1))
    ]
    held = pl.pallas_call(
        functools.partial(turn_kernel, n),
        out_shape=jax.ShapeDtypeStruct((rows, width), f32),
        in_specs=[HBM] * 3,
        out_specs=VMEM,
        scratch_shapes=[
            everything, everything, cut, cut, cut, cut, pltpu.VMEM((1, width), jnp.int32),
            pltpu.SMEM((ROUNDS - 1,), jnp.int32),
            pltpu.VMEM((2, 8, width), f32), pltpu.VMEM((8, width), f32),
            whole, part, part, part, pltpu.VMEM((2, 2, n // 2, share, width), f32), square, turn, turn,
            pltpu.VMEM((5, BW, BW), f32),
            whole, part, part, part, one, one, whole,
            pltpu.VMEM((2 * width, width), jnp.bfloat16), pltpu.VMEM((2 * width, width), jnp.bfloat16),
            dma((2 * CHUNKS,)), dma((2 * CHUNKS,)),
            dma((2, n // 2)), dma((2, n // 2)), dma((3, n // 2)), dma((3, n // 2)),
            dma((5,)), dma((5,)), dma((3,)), dma((3,)),
            dma((LOADS,)), dma((2,)),
        ],
        compiler_params=pltpu.CompilerParams(
            collective_id=0, has_side_effects=True, vmem_limit_bytes=40 * 1024 * 1024
        ),
    )(*operands)
    return pl.pallas_call(
        write_kernel,
        out_shape=jax.ShapeDtypeStruct((rows, width), f32),
        in_specs=[VMEM],
        out_specs=ANY,
        scratch_shapes=[dma((WRITES,))],
        compiler_params=pltpu.CompilerParams(vmem_limit_bytes=8 * 1024 * 1024),
    )(held)


def solution(mesh):
    placed = (P("rows", "blk"), P("blk"), P(None, "blk"))
    n = mesh.shape["rows"]
    pairs = mesh.shape["blk"] == 2 and n % 2 == 0 and (2 * BW) % (8 * n) == 0
    body = functools.partial(pair_body, n) if pairs else general_body
    return jax.shard_map(
        body, mesh=mesh, in_specs=placed, out_specs=P("rows", "blk"), check_vma=False
    )
```

```python
import functools

import jax
import jax.numpy as jnp
from jax import lax
from jax.experimental import pallas as pl
from jax.experimental.pallas import tpu as pltpu
from jax.sharding import PartitionSpec as P

BW = 128
ROUNDS = 4
NS_STEPS = 3
CHUNKS = 8
FIRST = 4
SOON = 3
TALL = 2
LOADS = 4
AFTER = 2

epsilon = 1e-06
relaxation = 1.2

MESH = pl.DeviceIdType.MESH
ROWS_DIM = (((0,), (0,)), ((), ()))
PLAIN = (((1,), (0,)), ((), ()))
VMEM = pl.BlockSpec(memory_space=pltpu.VMEM)
ANY = pl.BlockSpec(memory_space=pl.ANY)
HBM = pl.BlockSpec(memory_space=pltpu.HBM)


def from_behind(value, axis, by):
    peers = lax.axis_size(axis)
    return lax.ppermute(value, axis, [(i, (i + by) % peers) for i in range(peers)])


def rotation(cross_gram, squares, labels):
    left_scale = lax.rsqrt(squares[:BW] + epsilon)
    right_scale = lax.rsqrt(squares[BW:] + epsilon)
    grade_gap = jnp.abs(labels[:BW, None] - labels[None, BW:])
    scaled = cross_gram * left_scale[:, None] * right_scale[None, :] / (1.0 + grade_gap)
    magnitude = jnp.sqrt(jnp.sum(scaled * scaled) + epsilon)
    generator = relaxation * scaled / magnitude
    zeros_block = jnp.zeros_like(generator)
    upper_half = jnp.concatenate([zeros_block, generator], 1)
    lower_half = jnp.concatenate([-generator.T, zeros_block], 1)
    iterate = jnp.eye(2 * BW, dtype=generator.dtype) + jnp.concatenate([upper_half, lower_half], 0)
    for sweep in range(NS_STEPS):
        product = lax.dot_general(iterate, iterate, ROWS_DIM, precision=lax.Precision.HIGHEST)
        iterate = 1.5 * iterate - 0.5 * jnp.dot(iterate, product, precision=lax.Precision.HIGHEST)
    return iterate


def statistics(blocks):
    cross_part = lax.dot_general(
        blocks[:, :BW], blocks[:, BW:], ROWS_DIM, precision=lax.Precision.HIGHEST
    )
    square_part = jnp.sum(blocks * blocks, axis=0)
    return lax.psum((cross_part, square_part), "rows")


def assemble(first, incoming, staying):
    return jnp.where(
        first, jnp.concatenate([incoming, staying], -1), jnp.concatenate([staying, incoming], -1)
    )


def general_body(snapshots, grades, mover):
    blocks = snapshots
    labels = grades.astype(jnp.float32)
    for round_index in range(ROUNDS):
        cross_gram, squares = statistics(blocks)
        rotator = rotation(cross_gram, squares, labels)
        blocks = jnp.dot(blocks, rotator, precision=lax.Precision.HIGHEST)
        if round_index + 1 < ROUNDS:
            first = mover[round_index, 0] == 0
            move_label = jnp.where(first, labels[:BW], labels[BW:])
            stay_label = jnp.where(first, labels[BW:], labels[:BW])
            moving = jnp.where(first, blocks[:, :BW], blocks[:, BW:])
            staying = jnp.where(first, blocks[:, BW:], blocks[:, :BW])
            incoming, came_label = from_behind((moving, move_label), "blk", 1)
            blocks = assemble(first, incoming, staying)
            labels = assemble(first, came_label, stay_label)
    return blocks


def split(value):
    high = value.astype(jnp.bfloat16)
    return high, (value - high.astype(jnp.float32)).astype(jnp.bfloat16)


def dot_split(a, b, dims=PLAIN):
    (ah, al), (bh, bl) = a, b
    mul = functools.partial(lax.dot_general, dimension_numbers=dims, preferred_element_type=jnp.float32)
    return mul(ah, bh) + (mul(ah, bl) + mul(al, bh))


def dot3(a, b, dims=PLAIN):
    return dot_split(split(a), split(b), dims)


def dot6(a, b, dims=PLAIN):
    return lax.dot_general(
        a, b, dims, precision=lax.Precision.HIGHEST, preferred_element_type=jnp.float32
    )


def turn_kernel(
    n, x_hbm, grade_hbm, mover_hbm, held_ref, high_ref, low_ref, last_high, last_low,
    x_ref, near_ref, x_high, x_low, near_high, near_low, grade_ref, mover_ref, meta_ref, meta,
    dpart, dgot, dmid, dnear, dall, diag_ref, turn_ref, flip_ref, fac_ref,
    cpart, cgot, cmid, cnear, cmine, cother, cfull,
    x_send, x_recv, rs_send, rs_recv, ag_send, ag_recv, sib_send, sib_recv, one_send, one_recv,
    load_sem, side_sem,
):
    pos, me = lax.axis_index("blk"), lax.axis_index("rows")
    other = 1 - pos
    core, group = lax.rem(me, 2), me // 2
    groups = n // 2
    rows, width = x_ref.shape
    half = rows // 2
    piece = half // CHUNKS
    share = width // n
    partner, sibling = (other, me), (pos, me + 1 - 2 * core)
    peers = [None] + [lax.rem(group + k, groups) for k in range(1, groups)]

    loads = []
    for i in range(LOADS):
        part = pl.ds(i * (rows // LOADS), rows // LOADS)
        loads.append(pltpu.make_async_copy(x_hbm.at[part], x_ref.at[part], load_sem.at[i]))
    sides = [
        pltpu.make_async_copy(grade_hbm, grade_ref, side_sem.at[0]),
        pltpu.make_async_copy(mover_hbm, mover_ref, side_sem.at[1]),
    ]
    for copy in sides + loads:
        copy.start()
    barrier = pltpu.get_barrier_semaphore()
    for device in (partner, sibling):
        pl.semaphore_signal(barrier, inc=1, device_id=device, device_id_type=MESH)
    for peer in peers[1:]:
        pl.semaphore_signal(barrier, inc=1, device_id=(pos, 2 * peer + core), device_id_type=MESH)
    pl.semaphore_wait(barrier, groups + 1)

    def remote(src, dst, send, recv, device):
        copy = pltpu.make_async_remote_copy(
            src_ref=src, dst_ref=dst, send_sem=send, recv_sem=recv,
            device_id=device, device_id_type=MESH,
        )
        copy.start()
        return copy

    swaps = []
    for c in range(2 * CHUNKS):
        start = lax.rem(other * half + c * piece, rows)
        swaps.append(
            pltpu.make_async_remote_copy(
                src_ref=x_hbm.at[pl.ds(pl.multiple_of(start, piece), piece)],
                dst_ref=near_ref.at[pl.ds(c * piece, piece)],
                send_sem=x_send.at[c], recv_sem=x_recv.at[c],
                device_id=partner, device_id_type=MESH,
            )
        )

    def send(first, last):
        for c in range(first, last):
            swaps[c].start()

    send(0, FIRST)
    for copy in sides:
        copy.wait()
    meta[...] = jnp.zeros_like(meta)
    meta[0:1, :] = grade_ref[...].astype(jnp.float32)
    for r in range(ROUNDS - 1):
        meta[r + 1:r + 2, :] = jnp.full((1, width), mover_ref[r], jnp.int32).astype(jnp.float32)
    meta_ref[pos] = meta[...]
    labels = remote(meta, meta_ref.at[pos], one_send.at[0], one_recv.at[0], partner)

    def pair_up(part, got, which):
        return remote(part.at[1 - core], got, sib_send.at[which], sib_recv.at[which], sibling)

    def scatter(mid, near, which):
        return [
            remote(
                mid.at[peers[k]], near.at[k], rs_send.at[which, k], rs_recv.at[which, k],
                (pos, 2 * peers[k] + core),
            )
            for k in range(1, groups)
        ]

    def rotated(pair, p):
        return split(dot_split(pair, (turn_ref[p, 0], turn_ref[p, 1])))

    def summed(mid, near, copies):
        total = mid[group]
        for k in range(1, groups):
            copies[k - 1].wait()
            total = total + near[k]
        return total

    def gather(full, which):
        return [
            remote(
                full.at[core, group], full.at[core, group], ag_send.at[which, k],
                ag_recv.at[which, k], (pos, 2 * peers[k] + core),
            )
            for k in range(1, groups)
        ]

    def hand_over(full, copies, which):
        for copy in copies:
            copy.wait()
        return remote(full.at[core], full.at[core], sib_send.at[which], sib_recv.at[which], sibling)

    def receive(c):
        swaps[c].wait()
        there = slice(c * piece, (c + 1) * piece)
        near_high[there, :], near_low[there, :] = split(near_ref[there, :])

    def cross(c):
        receive(c)
        here = pl.ds(pl.multiple_of(pos * half + c * piece, piece), piece)
        there = slice(c * piece, (c + 1) * piece)
        mine = x_high[here, :], x_low[here, :]
        theirs = near_high[there, :], near_low[there, :]
        left = [jnp.where(pos == 0, a, b) for a, b in zip(mine, theirs)]
        right = [jnp.where(pos == 0, b, a) for a, b in zip(mine, theirs)]
        return dot_split(left, right, ROWS_DIM)

    both = jnp.zeros((width, 2 * width), jnp.float32)
    for i in range(LOADS):
        loads[i].wait()
        part = slice(i * (rows // LOADS), (i + 1) * (rows // LOADS))
        high, low = split(x_ref[part, :])
        x_high[part, :] = high
        x_low[part, :] = low
        both = both + lax.dot_general(
            high, jnp.concatenate([high, low], 1), ROWS_DIM, preferred_element_type=jnp.float32
        )
    own = both[:, :width] + (both[:, width:] + both[:, width:].T)
    dpart[...] = own.reshape(2, groups, share, width)
    copy = pair_up(dpart, dgot, 0)
    copy.wait()
    dmid[...] = dpart[core] + dgot[...]
    copies = scatter(dmid, dnear, 0)
    total = cross(0)
    dall[pos, core, group] = summed(dmid, dnear, copies)
    mine, theirs = dall.at[pos], dall.at[other]
    here = mine.at[core, group]
    d_swap = remote(here, here, one_send.at[1], one_recv.at[1], partner)
    own_copies = gather(mine, 0)
    send(FIRST, CHUNKS + SOON)
    total = total + cross(1)
    d_swap.wait()
    their_copies = gather(theirs, 1)
    own_copy = hand_over(mine, own_copies, 1)
    total = total + cross(2)

    def begin_round(p):
        begin(p, dall[p].reshape(width, width), meta_ref, turn_ref, flip_ref, diag_ref)

    own_copy.wait()
    begin_round(pos)
    their_copy = hand_over(theirs, their_copies, 2)
    total = total + cross(3)
    labels.wait()
    their_copy.wait()
    begin_round(other)
    for c in range(4, CHUNKS - 1):
        total = total + cross(c)
    last = CHUNKS - 1
    here = pl.ds(pl.multiple_of(pos * half + last * piece, piece), piece)
    mine = rotated((x_high[here, :], x_low[here, :]), pos)
    left = flip_ref[0, 0], flip_ref[0, 1]
    right = turn_ref[1, 0], turn_ref[1, 1]
    total = dot_split(left, split(dot_split(split(total), right)))
    receive(last)
    there = slice(last * piece, (last + 1) * piece)
    theirs = rotated((near_high[there, :], near_low[there, :]), other)
    left = [jnp.where(pos == 0, a, b) for a, b in zip(mine, theirs)]
    right = [jnp.where(pos == 0, b, a) for a, b in zip(mine, theirs)]
    total = total + dot_split(left, right, ROWS_DIM)
    cpart[...] = total.reshape(2, groups, share, width)
    copy = pair_up(cpart, cgot, 3)
    copy.wait()
    cmid[...] = cpart[core] + cgot[...]
    copies = scatter(cmid, cnear, 1)
    prepare(pos, meta_ref, diag_ref, fac_ref)
    cmine[...] = summed(cmid, cnear, copies)
    c_swap = remote(cmine, cother, one_send.at[2], one_recv.at[2], partner)
    send(CHUNKS + SOON, 2 * CHUNKS)
    c_swap.wait()
    cfull[core, group] = cmine[...] + cother[...]
    copies = gather(cfull, 2)
    hand_over(cfull, copies, 4).wait()
    chain(
        pos, cfull[...].reshape(width, width), diag_ref, turn_ref, flip_ref, meta_ref, fac_ref,
        high_ref, low_ref,
    )
    tile = TALL * piece
    for t in range(rows // tile):
        for c in range(max(t * TALL, CHUNKS), (t + 1) * TALL):
            receive(c)
        here = pl.ds(pl.multiple_of(lax.rem(pos * half + t * tile, rows), tile), tile)
        there = slice(t * tile, (t + 1) * tile)
        high = jnp.concatenate([x_high[here, :], near_high[there, :]], 1)
        low = jnp.concatenate([x_low[here, :], near_low[there, :]], 1)
        late = t - (rows // tile - AFTER)
        if late < 0:
            held_ref[there, :] = dot_split((high, low), (high_ref[...], low_ref[...]))
        else:
            after = slice(late * tile, (late + 1) * tile)
            last_high[after, :] = high
            last_low[after, :] = low


def eye(n):
    return (
        lax.broadcasted_iota(jnp.int32, (n, n), 0) == lax.broadcasted_iota(jnp.int32, (n, n), 1)
    ).astype(jnp.float32)


def cut3(value):
    high, rest = value.astype(jnp.bfloat16), None
    rest = value - high.astype(jnp.float32)
    middle = rest.astype(jnp.bfloat16)
    return high, middle, (rest - middle.astype(jnp.float32)).astype(jnp.bfloat16)


def mul(a, b, dims=PLAIN):
    return lax.dot_general(a, b, dims, preferred_element_type=jnp.float32)


def fine_left(a, b):
    (ah, am, al), (bh, bl) = a, b
    return mul(ah, bh) + ((mul(ah, bl) + mul(am, bh)) + (mul(am, bl) + mul(al, bh)))


def fine_right(a, b):
    (ah, al), (bh, bm, bl) = a, b
    return mul(ah, bh) + ((mul(ah, bm) + mul(al, bh)) + (mul(al, bm) + mul(ah, bl)))


def rotate(crosses, signs, work=()):
    work = list(work)
    unit = eye(BW)
    both = range(2)
    each = range(len(crosses))
    total = [jnp.sum(h * h, keepdims=True) + epsilon for h in crosses]
    cut = [split(h) for h in crosses]
    flip = [split(h.T) for h in crosses]
    scale = [relaxation * relaxation / t for t in total]
    m = [[scale[i] * dot_split(cut[i], flip[i]), scale[i] * dot_split(flip[i], cut[i])] for i in each]
    b = [relaxation * lax.rsqrt(total[i]) * signs[i] * crosses[i] for i in each]
    bc = [split(v) for v in b]
    if work:
        work.pop(0)()
    mc = [[split(v) for v in pair] for pair in m]
    m2 = [[dot_split(v, v) for v in pair] for pair in mc]
    mb = [dot_split(mc[i][0], bc[i]) for i in each]
    if work:
        work.pop(0)()
    m2c = [[split(v) for v in pair] for pair in m2]
    m3 = [[dot_split(m2c[i][j], mc[i][j]) for j in both] for i in each]
    m4 = [[dot_split(v, v) for v in pair] for pair in m2c]
    m2b = [dot_split(m2c[i][0], bc[i]) for i in each]
    m3b = [dot_split(m2c[i][0], split(mb[i])) for i in each]
    if work:
        work.pop(0)()
    n = [[0.75 * m2[i][j] - 0.25 * m3[i][j] for j in both] for i in each]
    p = [
        [
            unit - 0.5 * m[i][j] + 0.375 * m2[i][j] - 0.3125 * m3[i][j] + 0.0625 * m4[i][j]
            for j in both
        ]
        for i in each
    ]
    nb = [split(0.75 * m2b[i] - 0.25 * m3b[i]) for i in each]
    nc = [[split(v) for v in pair] for pair in n]
    pc = [[split(v) for v in pair] for pair in p]
    u = [[split(dot_split(v, v)) for v in pair] for pair in nc]
    r = [[split(dot_split(pc[i][j], split(0.375 * unit + 0.125 * n[i][j]))) for j in both] for i in each]
    pb = [dot_split(pc[i][0], bc[i]) for i in each]
    nnb = [split(dot_split(nc[i][0], nb[i])) for i in each]
    if work:
        work.pop(0)()
    out = []
    for i in each:
        gain = [p[i][j] + dot_split(r[i][j], u[i][j]) for j in both]
        out.append((gain[0], pb[i] + dot_split(r[i][0], nnb[i]), gain[1]))
    for step in work:
        step()
    return out


def columns(q):
    upper, edge, lower = q
    return (
        split(jnp.concatenate([upper, -edge.T], 0)), split(jnp.concatenate([edge, lower], 0))
    )


def turned(q):
    upper, edge, lower = q
    return (
        split(jnp.concatenate([upper, -edge], 1)), split(jnp.concatenate([edge.T, lower], 1))
    )


def choose(flag, a, b):
    return tuple(jnp.where(flag, u, v) for u, v in zip(a, b))


def order(flag, pair):
    return choose(flag, pair[1], pair[0]), choose(flag, pair[0], pair[1])


def beside(a, b, axis=1):
    return tuple(jnp.concatenate([u, v], axis) for u, v in zip(a, b))


def plan(meta_ref):
    flags, signs, kept = [], [], [1.0, 1.0]
    labels = [[meta_ref[p, 0:1, :BW], meta_ref[p, 0:1, BW:]] for p in range(2)]
    names = []
    for r in range(ROUNDS - 1):
        first = [1.0 - meta_ref[p, r + 1:r + 2, :BW] for p in range(2)]
        flag = [jnp.abs(first[p] - kept[p]) < 0.5 for p in range(2)]
        kept = [1.0 - first[0], first[1]]
        labels = [
            [jnp.where(flag[p], labels[p][1], labels[p][0]), jnp.where(flag[p], labels[p][0], labels[p][1])]
            for p in range(2)
        ]
        labels = [[labels[0][0], labels[1][1]], [labels[0][1], labels[1][0]]]
        flags.append(flag)
        signs.append([2.0 * k - 1.0 for k in kept])
        names.append(labels)
    return flags, signs, names


def tall(row):
    return jnp.broadcast_to(row, (BW, BW)).T


def weight(pair):
    return 1.0 / (1.0 + jnp.abs(tall(pair[0]) - pair[1]))


def begin(p, diag, meta_ref, turn_ref, flip_ref, diag_ref):
    unit = eye(BW)
    labels = meta_ref[p, 0:1, :]
    left = jnp.sum(diag[:BW, :BW] * unit, axis=1, keepdims=True)
    right = jnp.sum(diag[BW:, BW:] * unit, axis=0, keepdims=True)
    scale = lax.rsqrt(left + epsilon) * lax.rsqrt(right + epsilon)
    cross = diag[:BW, BW:] * (scale * weight((labels[:, :BW], labels[:, BW:])))
    (q,) = rotate([cross], [1.0])
    flag = meta_ref[p, 1:2, :BW] < 0.5
    q_cut = beside(*order(flag, columns(q)))
    wide = jnp.concatenate([flag, flag], 1)
    flip = beside(*order(wide, turned(q)), 0)
    for k in range(2):
        turn_ref[p, k] = q_cut[k]
        flip_ref[p, k] = flip[k]
    diag_ref[p] = fine_right(flip, cut3(fine_left(cut3(diag), q_cut)))


def prepare(pos, meta_ref, diag_ref, fac_ref):
    unit = eye(BW)
    flags, signs, names = plan(meta_ref)

    def scales(p, s, axis):
        part = slice(s * BW, s * BW + BW)
        return lax.rsqrt(jnp.sum(diag_ref[p, part, part] * unit, axis=axis, keepdims=True) + epsilon)

    fac_ref[0] = weight(names[0][0]) * scales(0, 0, 1) * scales(1, 1, 0)
    fac_ref[1] = weight(names[0][1]) * scales(0, 1, 1) * scales(1, 0, 0)
    fac_ref[2] = weight(names[1][0])
    fac_ref[3] = weight(names[1][1])
    fac_ref[4] = weight([jnp.where(pos == 0, a, b) for a, b in zip(*names[2])])


def chain(pos, between, diag_ref, turn_ref, flip_ref, meta_ref, fac_ref, high_ref, low_ref):
    assert ROUNDS == 4
    flags, signs, _ = plan(meta_ref)
    low, top = slice(0, BW), slice(BW, 2 * BW)
    turn = [(turn_ref[p, 0], turn_ref[p, 1]) for p in range(2)]

    def part(pair, rows=slice(None), cols=slice(None)):
        return tuple(v[rows, cols] for v in pair)

    held = {}
    x0, x1 = between[low, top], between[top, low]
    held["stay"], held["move"] = between[low, low], between[top, top]
    qs = rotate([x0 * fac_ref[0], x1 * fac_ref[1]], signs[0])
    d0 = jnp.concatenate([
        jnp.concatenate([diag_ref[0, low, low], x0], 1),
        jnp.concatenate([x0.T, diag_ref[1, top, top]], 1),
    ], 0)
    d1 = jnp.concatenate([
        jnp.concatenate([diag_ref[0, top, top], x1], 1),
        jnp.concatenate([x1.T, diag_ref[1, low, low]], 1),
    ], 0)
    g = jnp.concatenate([
        jnp.concatenate([diag_ref[0, low, top], held["stay"]], 1),
        jnp.concatenate([held["move"].T, diag_ref[1, top, low]], 1),
    ], 0)
    small = eye(2 * BW)
    row0 = jnp.sum(d0 * small, axis=0, keepdims=True)
    tall1 = jnp.sum(d1 * small, axis=1, keepdims=True)
    d0, d1, g = split(d0 - row0 * small), split(d1 - tall1 * small), split(g)
    q = [beside(*order(flags[1][p], columns(qs[p]))) for p in range(2)]
    wide = [jnp.concatenate([flags[1][p]] * 2, 1) for p in range(2)]
    qt = [beside(*order(wide[p], turned(qs[p])), 0) for p in range(2)]

    def full(pair):
        return pair[0].astype(jnp.float32) + pair[1].astype(jnp.float32)

    mid = split(dot_split(g, q[1]))
    t0 = full(qt[0]) * row0 + dot_split(qt[0], d0)
    t1 = full(q[1]) * tall1 + dot_split(d1, q[1])
    x0 = dot_split(part(qt[0], low), part(mid, cols=top))
    x1 = dot_split(part(qt[0], top), part(mid, cols=low))

    sq0 = lax.rsqrt(jnp.sum(full(qt[0]) * t0, axis=1, keepdims=True) + epsilon)
    sq1 = lax.rsqrt(jnp.sum(full(q[1]) * t1, axis=0, keepdims=True) + epsilon)

    def rest0():
        held["stay"] = dot_split(part(qt[0], low), part(mid, cols=low))
        held["move"] = dot_split(part(qt[0], top), part(mid, cols=top))
        held["d0"] = fine_left(cut3(t0), q[0])

    def rest1():
        held["d1"] = fine_right(qt[1], cut3(t1))
        held["w00"] = dot_split(part(turn[0], cols=low), part(q[0], low))

    def rest2():
        held["w01"] = dot_split(part(turn[1], cols=top), part(q[0], top))
        held["w10"] = dot_split(part(turn[0], cols=top), part(q[1], low))

    def rest3():
        held["w11"] = dot_split(part(turn[1], cols=low), part(q[1], top))

    qs = rotate(
        [x0 * (fac_ref[2] * sq0[low] * sq1[:, top]), x1 * (fac_ref[3] * sq0[top] * sq1[:, low])],
        signs[1], [rest0, rest1, rest2, rest3],
    )
    e0, e1 = held["d0"], held["d1"]
    d0 = split(jnp.concatenate([
        jnp.concatenate([e0[low, low], x0], 1), jnp.concatenate([x0.T, e1[top, top]], 1),
    ], 0))
    d1 = split(jnp.concatenate([
        jnp.concatenate([e0[top, top], x1], 1), jnp.concatenate([x1.T, e1[low, low]], 1),
    ], 0))
    g = split(jnp.concatenate([
        jnp.concatenate([e0[low, top], held["stay"]], 1),
        jnp.concatenate([held["move"].T, e1[top, low]], 1),
    ], 0))
    mine = pos == 0
    wide = jnp.concatenate([flags[2][0]] * 2, 1)
    stay, move = order(wide, turned(qs[0]))
    up = choose(mine, stay, move)
    stay, move = order(flags[2][0], columns(qs[0]))
    upright = choose(mine, stay, move)
    stay, move = order(flags[2][1], columns(qs[1]))
    side = choose(mine, move, stay)
    mid = split(dot_split(g, side))
    t0 = dot_split(up, d0)
    t1 = dot_split(d1, side)
    x = dot_split(up, mid)
    sq0 = lax.rsqrt(jnp.sum(full(up) * t0, axis=1, keepdims=True) + epsilon)
    sq1 = lax.rsqrt(jnp.sum(full(side) * t1, axis=0, keepdims=True) + epsilon)
    rows = [None, None]

    def tail(r):
        def run():
            a, b = held["w0" + str(r)], held["w1" + str(r)]
            first = split(jnp.concatenate([a[:, low], b[:, top]], 1))
            second = split(jnp.concatenate([a[:, top], b[:, low]], 1))
            rows[r] = split(jnp.concatenate([dot_split(first, upright), dot_split(second, side)], 1))
        return run

    sign = jnp.where(mine, signs[2][0], signs[2][1])
    (last,) = rotate([x * (fac_ref[4] * sq0 * sq1)], [sign], [tail(0), tail(1)])
    a, b = columns(last)
    last = beside(choose(sign > 0.0, a, b), choose(sign > 0.0, b, a))
    out = [split(dot_split(rows[r], last)) for r in range(2)]
    width = 2 * BW
    for p in range(2):
        high, lower = choose(mine, out[p], out[1 - p])
        high_ref[p * width:(p + 1) * width] = high
        low_ref[p * width:(p + 1) * width] = lower


def write_kernel(tile, held_ref, high_ref, low_ref, last_high, last_low, out_ref, made, sems):
    early, rows = held_ref.shape[0], out_ref.shape[0]
    pos = lax.axis_index("blk")
    copies = []

    def write(t, source):
        there = pl.ds(pl.multiple_of(lax.rem(pos * (rows // 2) + t * tile, rows), tile), tile)
        copies.append(pltpu.make_async_copy(source, out_ref.at[there], sems.at[t]))
        copies[-1].start()

    for t in range(early // tile):
        write(t, held_ref.at[pl.ds(t * tile, tile)])
    for t in range(early // tile, rows // tile):
        here = slice(t * tile - early, (t + 1) * tile - early)
        made[here, :] = dot_split((last_high[here, :], last_low[here, :]), (high_ref[...], low_ref[...]))
        write(t, made.at[pl.ds(t * tile - early, tile)])
    for copy in copies:
        copy.wait()


def pair_body(n, snapshots, grades, mover):
    rows, width = snapshots.shape
    share = width // n
    f32 = jnp.float32
    dma = pltpu.SemaphoreType.DMA
    whole = pltpu.VMEM((2, n // 2, share, width), f32)
    part = pltpu.VMEM((n // 2, share, width), f32)
    one = pltpu.VMEM((share, width), f32)
    everything = pltpu.VMEM((rows, width), f32)
    cut = pltpu.VMEM((rows, width), jnp.bfloat16)
    square = pltpu.VMEM((2, width, width), f32)
    turn = pltpu.VMEM((2, 2, width, width), jnp.bfloat16)
    operands = [
        pltpu.with_memory_space_constraint(value, pltpu.HBM)
        for value in (snapshots, grades.reshape(1, width), mover.reshape(ROUNDS - 1))
    ]
    tile = TALL * (rows // 2 // CHUNKS)
    late = AFTER * tile
    bf16 = jnp.bfloat16
    made = pl.pallas_call(
        functools.partial(turn_kernel, n),
        out_shape=(
            jax.ShapeDtypeStruct((rows - late, width), f32),
            jax.ShapeDtypeStruct((2 * width, width), bf16),
            jax.ShapeDtypeStruct((2 * width, width), bf16),
            jax.ShapeDtypeStruct((late, 2 * width), bf16),
            jax.ShapeDtypeStruct((late, 2 * width), bf16),
        ),
        in_specs=[HBM] * 3,
        out_specs=(VMEM,) * 5,
        scratch_shapes=[
            everything, everything, cut, cut, cut, cut, pltpu.VMEM((1, width), jnp.int32),
            pltpu.SMEM((ROUNDS - 1,), jnp.int32),
            pltpu.VMEM((2, 8, width), f32), pltpu.VMEM((8, width), f32),
            whole, part, part, part, pltpu.VMEM((2, 2, n // 2, share, width), f32), square, turn, turn,
            pltpu.VMEM((5, BW, BW), f32),
            whole, part, part, part, one, one, whole,
            dma((2 * CHUNKS,)), dma((2 * CHUNKS,)),
            dma((2, n // 2)), dma((2, n // 2)), dma((3, n // 2)), dma((3, n // 2)),
            dma((5,)), dma((5,)), dma((3,)), dma((3,)),
            dma((LOADS,)), dma((2,)),
        ],
        compiler_params=pltpu.CompilerParams(
            collective_id=0, has_side_effects=True, vmem_limit_bytes=40 * 1024 * 1024
        ),
    )(*operands)
    return pl.pallas_call(
        functools.partial(write_kernel, tile),
        out_shape=jax.ShapeDtypeStruct((rows, width), f32),
        in_specs=[VMEM] * 5,
        out_specs=ANY,
        scratch_shapes=[pltpu.VMEM((late, width), f32), dma((rows // tile,))],
        compiler_params=pltpu.CompilerParams(vmem_limit_bytes=8 * 1024 * 1024),
    )(*made)


def solution(mesh):
    placed = (P("rows", "blk"), P("blk"), P(None, "blk"))
    n = mesh.shape["rows"]
    pairs = mesh.shape["blk"] == 2 and n % 2 == 0 and (2 * BW) % (8 * n) == 0
    body = functools.partial(pair_body, n) if pairs else general_body
    return jax.shard_map(
        body, mesh=mesh, in_specs=placed, out_specs=P("rows", "blk"), check_vma=False
    )
```

```python
import functools

import jax
import jax.numpy as jnp
from jax import lax
from jax.experimental import pallas as pl
from jax.experimental.pallas import tpu as pltpu
from jax.sharding import PartitionSpec as P

BW = 128
ROUNDS = 4
NS_STEPS = 3
CHUNKS = 8
FIRST = 3
SOON = 3
TALL = 2
LOADS = 4
AFTER = 2

epsilon = 1e-06
relaxation = 1.2

MESH = pl.DeviceIdType.MESH
ROWS_DIM = (((0,), (0,)), ((), ()))
PLAIN = (((1,), (0,)), ((), ()))
VMEM = pl.BlockSpec(memory_space=pltpu.VMEM)
ANY = pl.BlockSpec(memory_space=pl.ANY)
HBM = pl.BlockSpec(memory_space=pltpu.HBM)


def from_behind(value, axis, by):
    peers = lax.axis_size(axis)
    return lax.ppermute(value, axis, [(i, (i + by) % peers) for i in range(peers)])


def rotation(cross_gram, squares, labels):
    left_scale = lax.rsqrt(squares[:BW] + epsilon)
    right_scale = lax.rsqrt(squares[BW:] + epsilon)
    grade_gap = jnp.abs(labels[:BW, None] - labels[None, BW:])
    scaled = cross_gram * left_scale[:, None] * right_scale[None, :] / (1.0 + grade_gap)
    magnitude = jnp.sqrt(jnp.sum(scaled * scaled) + epsilon)
    generator = relaxation * scaled / magnitude
    zeros_block = jnp.zeros_like(generator)
    upper_half = jnp.concatenate([zeros_block, generator], 1)
    lower_half = jnp.concatenate([-generator.T, zeros_block], 1)
    iterate = jnp.eye(2 * BW, dtype=generator.dtype) + jnp.concatenate([upper_half, lower_half], 0)
    for sweep in range(NS_STEPS):
        product = lax.dot_general(iterate, iterate, ROWS_DIM, precision=lax.Precision.HIGHEST)
        iterate = 1.5 * iterate - 0.5 * jnp.dot(iterate, product, precision=lax.Precision.HIGHEST)
    return iterate


def statistics(blocks):
    cross_part = lax.dot_general(
        blocks[:, :BW], blocks[:, BW:], ROWS_DIM, precision=lax.Precision.HIGHEST
    )
    square_part = jnp.sum(blocks * blocks, axis=0)
    return lax.psum((cross_part, square_part), "rows")


def assemble(first, incoming, staying):
    return jnp.where(
        first, jnp.concatenate([incoming, staying], -1), jnp.concatenate([staying, incoming], -1)
    )


def general_body(snapshots, grades, mover):
    blocks = snapshots
    labels = grades.astype(jnp.float32)
    for round_index in range(ROUNDS):
        cross_gram, squares = statistics(blocks)
        rotator = rotation(cross_gram, squares, labels)
        blocks = jnp.dot(blocks, rotator, precision=lax.Precision.HIGHEST)
        if round_index + 1 < ROUNDS:
            first = mover[round_index, 0] == 0
            move_label = jnp.where(first, labels[:BW], labels[BW:])
            stay_label = jnp.where(first, labels[BW:], labels[:BW])
            moving = jnp.where(first, blocks[:, :BW], blocks[:, BW:])
            staying = jnp.where(first, blocks[:, BW:], blocks[:, :BW])
            incoming, came_label = from_behind((moving, move_label), "blk", 1)
            blocks = assemble(first, incoming, staying)
            labels = assemble(first, came_label, stay_label)
    return blocks


def split(value):
    high = value.astype(jnp.bfloat16)
    return high, (value - high.astype(jnp.float32)).astype(jnp.bfloat16)


def dot_split(a, b, dims=PLAIN):
    (ah, al), (bh, bl) = a, b
    mul = functools.partial(lax.dot_general, dimension_numbers=dims, preferred_element_type=jnp.float32)
    return mul(ah, bh) + (mul(ah, bl) + mul(al, bh))


def dot3(a, b, dims=PLAIN):
    return dot_split(split(a), split(b), dims)


def dot6(a, b, dims=PLAIN):
    return lax.dot_general(
        a, b, dims, precision=lax.Precision.HIGHEST, preferred_element_type=jnp.float32
    )


def turn_kernel(
    n, x_hbm, grade_hbm, mover_hbm, held_ref, high_ref, low_ref, last_high, last_low,
    x_ref, near_ref, x_high, x_low, near_high, near_low, grade_ref, mover_ref, meta_ref, meta,
    dpart, dgot, dmid, dnear, dall, diag_ref, turn_ref, flip_ref, fac_ref,
    cpart, cgot, cmid, cnear, cmine, cother, cfull,
    x_send, x_recv, rs_send, rs_recv, ag_send, ag_recv, sib_send, sib_recv, one_send, one_recv,
    load_sem, side_sem, ready_sem,
):
    pos, me = lax.axis_index("blk"), lax.axis_index("rows")
    other = 1 - pos
    core, group = lax.rem(me, 2), me // 2
    groups = n // 2
    rows, width = x_ref.shape
    half = rows // 2
    piece = half // CHUNKS
    share = width // n
    partner, sibling = (other, me), (pos, me + 1 - 2 * core)
    peers = [None] + [lax.rem(group + k, groups) for k in range(1, groups)]

    barrier = pltpu.get_barrier_semaphore()
    for peer in peers[1:]:
        pl.semaphore_signal(barrier, inc=1, device_id=(pos, 2 * peer + 1), device_id_type=MESH)
    for device in ((other, me - core), sibling):
        pl.semaphore_signal(barrier, inc=1, device_id=device, device_id_type=MESH)
    loads = []
    for i in range(LOADS):
        part = pl.ds(i * (rows // LOADS), rows // LOADS)
        loads.append(pltpu.make_async_copy(x_hbm.at[part], x_ref.at[part], load_sem.at[i]))
    sides = [
        pltpu.make_async_copy(grade_hbm, grade_ref, side_sem.at[0]),
        pltpu.make_async_copy(mover_hbm, mover_ref, side_sem.at[1]),
    ]
    for copy in sides + loads:
        copy.start()

    def relay(source):
        @pl.when(core == source)
        def _():
            pl.semaphore_signal(ready_sem, inc=1, device_id=sibling, device_id_type=MESH)

        @pl.when(core != source)
        def _():
            pl.semaphore_wait(ready_sem, 1)

    @pl.when(core == 0)
    def _():
        pl.semaphore_wait(barrier, 3)

    relay(0)

    def remote(src, dst, send, recv, device):
        copy = pltpu.make_async_remote_copy(
            src_ref=src, dst_ref=dst, send_sem=send, recv_sem=recv,
            device_id=device, device_id_type=MESH,
        )
        copy.start()
        return copy

    swaps = []
    for c in range(2 * CHUNKS):
        start = lax.rem(other * half + c * piece, rows)
        swaps.append(
            pltpu.make_async_remote_copy(
                src_ref=x_hbm.at[pl.ds(pl.multiple_of(start, piece), piece)],
                dst_ref=near_ref.at[pl.ds(c * piece, piece)],
                send_sem=x_send.at[c], recv_sem=x_recv.at[c],
                device_id=partner, device_id_type=MESH,
            )
        )

    def send(first, last):
        for c in range(first, last):
            swaps[c].start()

    send(0, FIRST)
    for copy in sides:
        copy.wait()
    meta[...] = jnp.zeros_like(meta)
    meta[0:1, :] = grade_ref[...].astype(jnp.float32)
    for r in range(ROUNDS - 1):
        meta[r + 1:r + 2, :] = jnp.full((1, width), mover_ref[r], jnp.int32).astype(jnp.float32)
    meta_ref[pos] = meta[...]
    labels = remote(meta, meta_ref.at[pos], one_send.at[0], one_recv.at[0], partner)

    def pair_up(part, got, which):
        return remote(part.at[1 - core], got, sib_send.at[which], sib_recv.at[which], sibling)

    def scatter(mid, near, which):
        return [
            remote(
                mid.at[peers[k]], near.at[k], rs_send.at[which, k], rs_recv.at[which, k],
                (pos, 2 * peers[k] + core),
            )
            for k in range(1, groups)
        ]

    def rotated(pair, p):
        return split(dot_split(pair, (turn_ref[p, 0], turn_ref[p, 1])))

    def summed(mid, near, copies):
        total = mid[group]
        for k in range(1, groups):
            copies[k - 1].wait()
            total = total + near[k]
        return total

    def gather(full, which):
        return [
            remote(
                full.at[core, group], full.at[core, group], ag_send.at[which, k],
                ag_recv.at[which, k], (pos, 2 * peers[k] + core),
            )
            for k in range(1, groups)
        ]

    def hand_over(full, copies, which):
        for copy in copies:
            copy.wait()
        return remote(full.at[core], full.at[core], sib_send.at[which], sib_recv.at[which], sibling)

    def receive(c):
        swaps[c].wait()
        there = slice(c * piece, (c + 1) * piece)
        near_high[there, :], near_low[there, :] = split(near_ref[there, :])

    def cross(c):
        receive(c)
        here = pl.ds(pl.multiple_of(pos * half + c * piece, piece), piece)
        there = slice(c * piece, (c + 1) * piece)
        mine = x_high[here, :], x_low[here, :]
        theirs = near_high[there, :], near_low[there, :]
        left = [jnp.where(pos == 0, a, b) for a, b in zip(mine, theirs)]
        right = [jnp.where(pos == 0, b, a) for a, b in zip(mine, theirs)]
        return dot_split(left, right, ROWS_DIM)

    both = jnp.zeros((width, 2 * width), jnp.float32)
    for i in range(LOADS):
        loads[i].wait()
        part = slice(i * (rows // LOADS), (i + 1) * (rows // LOADS))
        high, low = split(x_ref[part, :])
        x_high[part, :] = high
        x_low[part, :] = low
        both = both + lax.dot_general(
            high, jnp.concatenate([high, low], 1), ROWS_DIM, preferred_element_type=jnp.float32
        )
    own = both[:, :width] + (both[:, width:] + both[:, width:].T)
    dpart[...] = own.reshape(2, groups, share, width)
    copy = pair_up(dpart, dgot, 0)
    copy.wait()
    dmid[...] = dpart[core] + dgot[...]

    @pl.when(core == 1)
    def _():
        pl.semaphore_wait(barrier, 2 * groups - 1)

    relay(1)
    copies = scatter(dmid, dnear, 0)
    total = cross(0)
    dall[pos, core, group] = summed(dmid, dnear, copies)
    mine, theirs = dall.at[pos], dall.at[other]
    here = mine.at[core, group]
    d_swap = remote(here, here, one_send.at[1], one_recv.at[1], partner)
    own_copies = gather(mine, 0)
    send(FIRST, CHUNKS + SOON)
    total = total + cross(1)
    d_swap.wait()
    their_copies = gather(theirs, 1)
    own_copy = hand_over(mine, own_copies, 1)
    total = total + cross(2)

    def begin_round(p, work=()):
        begin(p, dall[p].reshape(width, width), meta_ref, turn_ref, flip_ref, diag_ref, work)

    own_copy.wait()
    handed = []

    def pass_on():
        handed.append(hand_over(theirs, their_copies, 2))

    begin_round(pos, [lambda: None, lambda: None, pass_on])
    total = total + cross(3)
    labels.wait()
    handed[0].wait()
    begin_round(other)
    for c in range(4, CHUNKS - 1):
        total = total + cross(c)
    last = CHUNKS - 1
    here = pl.ds(pl.multiple_of(pos * half + last * piece, piece), piece)
    mine = rotated((x_high[here, :], x_low[here, :]), pos)
    left = flip_ref[0, 0], flip_ref[0, 1]
    right = turn_ref[1, 0], turn_ref[1, 1]
    total = dot_split(left, split(dot_split(split(total), right)))
    receive(last)
    there = slice(last * piece, (last + 1) * piece)
    theirs = rotated((near_high[there, :], near_low[there, :]), other)
    left = [jnp.where(pos == 0, a, b) for a, b in zip(mine, theirs)]
    right = [jnp.where(pos == 0, b, a) for a, b in zip(mine, theirs)]
    total = total + dot_split(left, right, ROWS_DIM)
    cpart[...] = total.reshape(2, groups, share, width)
    copy = pair_up(cpart, cgot, 3)
    copy.wait()
    cmid[...] = cpart[core] + cgot[...]
    copies = scatter(cmid, cnear, 1)
    prepare(pos, meta_ref, diag_ref, fac_ref)
    cmine[...] = summed(cmid, cnear, copies)
    c_swap = remote(cmine, cother, one_send.at[2], one_recv.at[2], partner)
    send(CHUNKS + SOON, 2 * CHUNKS)
    c_swap.wait()
    cfull[core, group] = cmine[...] + cother[...]
    copies = gather(cfull, 2)
    hand_over(cfull, copies, 4).wait()
    chain(
        pos, cfull[...].reshape(width, width), diag_ref, turn_ref, flip_ref, meta_ref, fac_ref,
        high_ref, low_ref,
    )
    tile = TALL * piece
    for t in range(rows // tile):
        for c in range(max(t * TALL, CHUNKS), (t + 1) * TALL):
            receive(c)
        here = pl.ds(pl.multiple_of(lax.rem(pos * half + t * tile, rows), tile), tile)
        there = slice(t * tile, (t + 1) * tile)
        high = jnp.concatenate([x_high[here, :], near_high[there, :]], 1)
        low = jnp.concatenate([x_low[here, :], near_low[there, :]], 1)
        late = t - (rows // tile - AFTER)
        if late < 0:
            held_ref[there, :] = dot_split((high, low), (high_ref[...], low_ref[...]))
        else:
            after = slice(late * tile, (late + 1) * tile)
            last_high[after, :] = high
            last_low[after, :] = low


def eye(n):
    return (
        lax.broadcasted_iota(jnp.int32, (n, n), 0) == lax.broadcasted_iota(jnp.int32, (n, n), 1)
    ).astype(jnp.float32)


def cut3(value):
    high, rest = value.astype(jnp.bfloat16), None
    rest = value - high.astype(jnp.float32)
    middle = rest.astype(jnp.bfloat16)
    return high, middle, (rest - middle.astype(jnp.float32)).astype(jnp.bfloat16)


def mul(a, b, dims=PLAIN):
    return lax.dot_general(a, b, dims, preferred_element_type=jnp.float32)


def fine_left(a, b):
    (ah, am, al), (bh, bl) = a, b
    return mul(ah, bh) + ((mul(ah, bl) + mul(am, bh)) + (mul(am, bl) + mul(al, bh)))


def fine_right(a, b):
    (ah, al), (bh, bm, bl) = a, b
    return mul(ah, bh) + ((mul(ah, bm) + mul(al, bh)) + (mul(al, bm) + mul(ah, bl)))


def rotate(crosses, signs, work=()):
    work = list(work)
    unit = eye(BW)
    both = range(2)
    each = range(len(crosses))
    total = [jnp.sum(h * h, keepdims=True) + epsilon for h in crosses]
    cut = [split(h) for h in crosses]
    flip = [split(h.T) for h in crosses]
    scale = [relaxation * relaxation / t for t in total]
    m = [[scale[i] * dot_split(cut[i], flip[i]), scale[i] * dot_split(flip[i], cut[i])] for i in each]
    b = [relaxation * lax.rsqrt(total[i]) * signs[i] * crosses[i] for i in each]
    bc = [split(v) for v in b]
    if work:
        work.pop(0)()
    mc = [[split(v) for v in pair] for pair in m]
    m2 = [[dot_split(v, v) for v in pair] for pair in mc]
    mb = [dot_split(mc[i][0], bc[i]) for i in each]
    if work:
        work.pop(0)()
    m2c = [[split(v) for v in pair] for pair in m2]
    m3 = [[dot_split(m2c[i][j], mc[i][j]) for j in both] for i in each]
    m4 = [[dot_split(v, v) for v in pair] for pair in m2c]
    m2b = [dot_split(m2c[i][0], bc[i]) for i in each]
    m3b = [dot_split(m2c[i][0], split(mb[i])) for i in each]
    if work:
        work.pop(0)()
    n = [[0.75 * m2[i][j] - 0.25 * m3[i][j] for j in both] for i in each]
    p = [
        [
            unit - 0.5 * m[i][j] + 0.375 * m2[i][j] - 0.3125 * m3[i][j] + 0.0625 * m4[i][j]
            for j in both
        ]
        for i in each
    ]
    nb = [split(0.75 * m2b[i] - 0.25 * m3b[i]) for i in each]
    nc = [[split(v) for v in pair] for pair in n]
    pc = [[split(v) for v in pair] for pair in p]
    u = [[split(dot_split(v, v)) for v in pair] for pair in nc]
    r = [[split(dot_split(pc[i][j], split(0.375 * unit + 0.125 * n[i][j]))) for j in both] for i in each]
    pb = [dot_split(pc[i][0], bc[i]) for i in each]
    nnb = [split(dot_split(nc[i][0], nb[i])) for i in each]
    if work:
        work.pop(0)()
    out = []
    for i in each:
        gain = [p[i][j] + dot_split(r[i][j], u[i][j]) for j in both]
        out.append((gain[0], pb[i] + dot_split(r[i][0], nnb[i]), gain[1]))
    for step in work:
        step()
    return out


def columns(q):
    upper, edge, lower = q
    return (
        split(jnp.concatenate([upper, -edge.T], 0)), split(jnp.concatenate([edge, lower], 0))
    )


def turned(q):
    upper, edge, lower = q
    return (
        split(jnp.concatenate([upper, -edge], 1)), split(jnp.concatenate([edge.T, lower], 1))
    )


def choose(flag, a, b):
    return tuple(jnp.where(flag, u, v) for u, v in zip(a, b))


def order(flag, pair):
    return choose(flag, pair[1], pair[0]), choose(flag, pair[0], pair[1])


def beside(a, b, axis=1):
    return tuple(jnp.concatenate([u, v], axis) for u, v in zip(a, b))


def plan(meta_ref):
    flags, signs, kept = [], [], [1.0, 1.0]
    labels = [[meta_ref[p, 0:1, :BW], meta_ref[p, 0:1, BW:]] for p in range(2)]
    names = []
    for r in range(ROUNDS - 1):
        first = [1.0 - meta_ref[p, r + 1:r + 2, :BW] for p in range(2)]
        flag = [jnp.abs(first[p] - kept[p]) < 0.5 for p in range(2)]
        kept = [1.0 - first[0], first[1]]
        labels = [
            [jnp.where(flag[p], labels[p][1], labels[p][0]), jnp.where(flag[p], labels[p][0], labels[p][1])]
            for p in range(2)
        ]
        labels = [[labels[0][0], labels[1][1]], [labels[0][1], labels[1][0]]]
        flags.append(flag)
        signs.append([2.0 * k - 1.0 for k in kept])
        names.append(labels)
    return flags, signs, names


def tall(row):
    return jnp.broadcast_to(row, (BW, BW)).T


def weight(pair):
    return 1.0 / (1.0 + jnp.abs(tall(pair[0]) - pair[1]))


def begin(p, diag, meta_ref, turn_ref, flip_ref, diag_ref, work=()):
    unit = eye(BW)
    labels = meta_ref[p, 0:1, :]
    left = jnp.sum(diag[:BW, :BW] * unit, axis=1, keepdims=True)
    right = jnp.sum(diag[BW:, BW:] * unit, axis=0, keepdims=True)
    scale = lax.rsqrt(left + epsilon) * lax.rsqrt(right + epsilon)
    cross = diag[:BW, BW:] * (scale * weight((labels[:, :BW], labels[:, BW:])))
    (q,) = rotate([cross], [1.0], work)
    flag = meta_ref[p, 1:2, :BW] < 0.5
    q_cut = beside(*order(flag, columns(q)))
    wide = jnp.concatenate([flag, flag], 1)
    flip = beside(*order(wide, turned(q)), 0)
    for k in range(2):
        turn_ref[p, k] = q_cut[k]
        flip_ref[p, k] = flip[k]
    diag_ref[p] = fine_right(flip, cut3(fine_left(cut3(diag), q_cut)))


def prepare(pos, meta_ref, diag_ref, fac_ref):
    unit = eye(BW)
    flags, signs, names = plan(meta_ref)

    def scales(p, s, axis):
        part = slice(s * BW, s * BW + BW)
        return lax.rsqrt(jnp.sum(diag_ref[p, part, part] * unit, axis=axis, keepdims=True) + epsilon)

    fac_ref[0] = weight(names[0][0]) * scales(0, 0, 1) * scales(1, 1, 0)
    fac_ref[1] = weight(names[0][1]) * scales(0, 1, 1) * scales(1, 0, 0)
    fac_ref[2] = weight(names[1][0])
    fac_ref[3] = weight(names[1][1])
    fac_ref[4] = weight([jnp.where(pos == 0, a, b) for a, b in zip(*names[2])])


def chain(pos, between, diag_ref, turn_ref, flip_ref, meta_ref, fac_ref, high_ref, low_ref):
    assert ROUNDS == 4
    flags, signs, _ = plan(meta_ref)
    low, top = slice(0, BW), slice(BW, 2 * BW)
    turn = [(turn_ref[p, 0], turn_ref[p, 1]) for p in range(2)]

    def part(pair, rows=slice(None), cols=slice(None)):
        return tuple(v[rows, cols] for v in pair)

    held = {}
    x0, x1 = between[low, top], between[top, low]
    held["stay"], held["move"] = between[low, low], between[top, top]
    qs = rotate([x0 * fac_ref[0], x1 * fac_ref[1]], signs[0])
    d0 = jnp.concatenate([
        jnp.concatenate([diag_ref[0, low, low], x0], 1),
        jnp.concatenate([x0.T, diag_ref[1, top, top]], 1),
    ], 0)
    d1 = jnp.concatenate([
        jnp.concatenate([diag_ref[0, top, top], x1], 1),
        jnp.concatenate([x1.T, diag_ref[1, low, low]], 1),
    ], 0)
    g = jnp.concatenate([
        jnp.concatenate([diag_ref[0, low, top], held["stay"]], 1),
        jnp.concatenate([held["move"].T, diag_ref[1, top, low]], 1),
    ], 0)
    small = eye(2 * BW)
    row0 = jnp.sum(d0 * small, axis=0, keepdims=True)
    tall1 = jnp.sum(d1 * small, axis=1, keepdims=True)
    d0, d1, g = split(d0 - row0 * small), split(d1 - tall1 * small), split(g)
    q = [beside(*order(flags[1][p], columns(qs[p]))) for p in range(2)]
    wide = [jnp.concatenate([flags[1][p]] * 2, 1) for p in range(2)]
    qt = [beside(*order(wide[p], turned(qs[p])), 0) for p in range(2)]

    def full(pair):
        return pair[0].astype(jnp.float32) + pair[1].astype(jnp.float32)

    mid = split(dot_split(g, q[1]))
    t0 = full(qt[0]) * row0 + dot_split(qt[0], d0)
    t1 = full(q[1]) * tall1 + dot_split(d1, q[1])
    x0 = dot_split(part(qt[0], low), part(mid, cols=top))
    x1 = dot_split(part(qt[0], top), part(mid, cols=low))

    sq0 = lax.rsqrt(jnp.sum(full(qt[0]) * t0, axis=1, keepdims=True) + epsilon)
    sq1 = lax.rsqrt(jnp.sum(full(q[1]) * t1, axis=0, keepdims=True) + epsilon)

    def rest0():
        held["stay"] = dot_split(part(qt[0], low), part(mid, cols=low))
        held["move"] = dot_split(part(qt[0], top), part(mid, cols=top))
        held["d0"] = fine_left(cut3(t0), q[0])

    def rest1():
        held["d1"] = fine_right(qt[1], cut3(t1))
        held["w00"] = dot_split(part(turn[0], cols=low), part(q[0], low))

    def rest2():
        held["w01"] = dot_split(part(turn[1], cols=top), part(q[0], top))
        held["w10"] = dot_split(part(turn[0], cols=top), part(q[1], low))

    def rest3():
        held["w11"] = dot_split(part(turn[1], cols=low), part(q[1], top))

    qs = rotate(
        [x0 * (fac_ref[2] * sq0[low] * sq1[:, top]), x1 * (fac_ref[3] * sq0[top] * sq1[:, low])],
        signs[1], [rest0, rest1, rest2, rest3],
    )
    e0, e1 = held["d0"], held["d1"]
    d0 = split(jnp.concatenate([
        jnp.concatenate([e0[low, low], x0], 1), jnp.concatenate([x0.T, e1[top, top]], 1),
    ], 0))
    d1 = split(jnp.concatenate([
        jnp.concatenate([e0[top, top], x1], 1), jnp.concatenate([x1.T, e1[low, low]], 1),
    ], 0))
    g = split(jnp.concatenate([
        jnp.concatenate([e0[low, top], held["stay"]], 1),
        jnp.concatenate([held["move"].T, e1[top, low]], 1),
    ], 0))
    mine = pos == 0
    wide = jnp.concatenate([flags[2][0]] * 2, 1)
    stay, move = order(wide, turned(qs[0]))
    up = choose(mine, stay, move)
    stay, move = order(flags[2][0], columns(qs[0]))
    upright = choose(mine, stay, move)
    stay, move = order(flags[2][1], columns(qs[1]))
    side = choose(mine, move, stay)
    mid = split(dot_split(g, side))
    t0 = dot_split(up, d0)
    t1 = dot_split(d1, side)
    x = dot_split(up, mid)
    sq0 = lax.rsqrt(jnp.sum(full(up) * t0, axis=1, keepdims=True) + epsilon)
    sq1 = lax.rsqrt(jnp.sum(full(side) * t1, axis=0, keepdims=True) + epsilon)
    rows = [None, None]

    def tail(r):
        def run():
            a, b = held["w0" + str(r)], held["w1" + str(r)]
            first = split(jnp.concatenate([a[:, low], b[:, top]], 1))
            second = split(jnp.concatenate([a[:, top], b[:, low]], 1))
            rows[r] = split(jnp.concatenate([dot_split(first, upright), dot_split(second, side)], 1))
        return run

    sign = jnp.where(mine, signs[2][0], signs[2][1])
    (last,) = rotate([x * (fac_ref[4] * sq0 * sq1)], [sign], [tail(0), tail(1)])
    a, b = columns(last)
    last = beside(choose(sign > 0.0, a, b), choose(sign > 0.0, b, a))
    out = [split(dot_split(rows[r], last)) for r in range(2)]
    width = 2 * BW
    for p in range(2):
        high, lower = choose(mine, out[p], out[1 - p])
        high_ref[p * width:(p + 1) * width] = high
        low_ref[p * width:(p + 1) * width] = lower


def write_kernel(tile, held_ref, high_ref, low_ref, last_high, last_low, out_ref, made, sems):
    early, rows = held_ref.shape[0], out_ref.shape[0]
    pos = lax.axis_index("blk")
    copies = []

    def write(t, source):
        there = pl.ds(pl.multiple_of(lax.rem(pos * (rows // 2) + t * tile, rows), tile), tile)
        copies.append(pltpu.make_async_copy(source, out_ref.at[there], sems.at[t]))
        copies[-1].start()

    for t in range(early // tile):
        write(t, held_ref.at[pl.ds(t * tile, tile)])
    for t in range(early // tile, rows // tile):
        here = slice(t * tile - early, (t + 1) * tile - early)
        made[here, :] = dot_split((last_high[here, :], last_low[here, :]), (high_ref[...], low_ref[...]))
        write(t, made.at[pl.ds(t * tile - early, tile)])
    for copy in copies:
        copy.wait()


def pair_body(n, snapshots, grades, mover):
    rows, width = snapshots.shape
    share = width // n
    f32 = jnp.float32
    dma = pltpu.SemaphoreType.DMA
    whole = pltpu.VMEM((2, n // 2, share, width), f32)
    part = pltpu.VMEM((n // 2, share, width), f32)
    one = pltpu.VMEM((share, width), f32)
    everything = pltpu.VMEM((rows, width), f32)
    cut = pltpu.VMEM((rows, width), jnp.bfloat16)
    square = pltpu.VMEM((2, width, width), f32)
    turn = pltpu.VMEM((2, 2, width, width), jnp.bfloat16)
    operands = [
        pltpu.with_memory_space_constraint(value, pltpu.HBM)
        for value in (snapshots, grades.reshape(1, width), mover.reshape(ROUNDS - 1))
    ]
    tile = TALL * (rows // 2 // CHUNKS)
    late = AFTER * tile
    bf16 = jnp.bfloat16
    made = pl.pallas_call(
        functools.partial(turn_kernel, n),
        out_shape=(
            jax.ShapeDtypeStruct((rows - late, width), f32),
            jax.ShapeDtypeStruct((2 * width, width), bf16),
            jax.ShapeDtypeStruct((2 * width, width), bf16),
            jax.ShapeDtypeStruct((late, 2 * width), bf16),
            jax.ShapeDtypeStruct((late, 2 * width), bf16),
        ),
        in_specs=[HBM] * 3,
        out_specs=(VMEM,) * 5,
        scratch_shapes=[
            everything, everything, cut, cut, cut, cut, pltpu.VMEM((1, width), jnp.int32),
            pltpu.SMEM((ROUNDS - 1,), jnp.int32),
            pltpu.VMEM((2, 8, width), f32), pltpu.VMEM((8, width), f32),
            whole, part, part, part, pltpu.VMEM((2, 2, n // 2, share, width), f32), square, turn, turn,
            pltpu.VMEM((5, BW, BW), f32),
            whole, part, part, part, one, one, whole,
            dma((2 * CHUNKS,)), dma((2 * CHUNKS,)),
            dma((2, n // 2)), dma((2, n // 2)), dma((3, n // 2)), dma((3, n // 2)),
            dma((5,)), dma((5,)), dma((3,)), dma((3,)),
            dma((LOADS,)), dma((2,)), pltpu.SemaphoreType.REGULAR,
        ],
        compiler_params=pltpu.CompilerParams(
            collective_id=0, has_side_effects=True, vmem_limit_bytes=40 * 1024 * 1024
        ),
    )(*operands)
    return pl.pallas_call(
        functools.partial(write_kernel, tile),
        out_shape=jax.ShapeDtypeStruct((rows, width), f32),
        in_specs=[VMEM] * 5,
        out_specs=ANY,
        scratch_shapes=[pltpu.VMEM((late, width), f32), dma((rows // tile,))],
        compiler_params=pltpu.CompilerParams(vmem_limit_bytes=8 * 1024 * 1024),
    )(*made)


def solution(mesh):
    placed = (P("rows", "blk"), P("blk"), P(None, "blk"))
    n = mesh.shape["rows"]
    pairs = mesh.shape["blk"] == 2 and n % 2 == 0 and (2 * BW) % (8 * n) == 0
    body = functools.partial(pair_body, n) if pairs else general_body
    return jax.shard_map(
        body, mesh=mesh, in_specs=placed, out_specs=P("rows", "blk"), check_vma=False
    )
```

```python
import functools

import jax
import jax.numpy as jnp
from jax import lax
from jax.experimental import pallas as pl
from jax.experimental.pallas import tpu as pltpu
from jax.sharding import PartitionSpec as P

BW = 128
ROUNDS = 4
NS_STEPS = 3
CHUNKS = 8
FIRST = 3
DIRECT = 1
SOON = 3
TALL = 2
LOADS = 4
AFTER = 4

epsilon = 1e-06
relaxation = 1.2

MESH = pl.DeviceIdType.MESH
ROWS_DIM = (((0,), (0,)), ((), ()))
PLAIN = (((1,), (0,)), ((), ()))
VMEM = pl.BlockSpec(memory_space=pltpu.VMEM)
ANY = pl.BlockSpec(memory_space=pl.ANY)
HBM = pl.BlockSpec(memory_space=pltpu.HBM)


def from_behind(value, axis, by):
    peers = lax.axis_size(axis)
    return lax.ppermute(value, axis, [(i, (i + by) % peers) for i in range(peers)])


def rotation(cross_gram, squares, labels):
    left_scale = lax.rsqrt(squares[:BW] + epsilon)
    right_scale = lax.rsqrt(squares[BW:] + epsilon)
    grade_gap = jnp.abs(labels[:BW, None] - labels[None, BW:])
    scaled = cross_gram * left_scale[:, None] * right_scale[None, :] / (1.0 + grade_gap)
    magnitude = jnp.sqrt(jnp.sum(scaled * scaled) + epsilon)
    generator = relaxation * scaled / magnitude
    zeros_block = jnp.zeros_like(generator)
    upper_half = jnp.concatenate([zeros_block, generator], 1)
    lower_half = jnp.concatenate([-generator.T, zeros_block], 1)
    iterate = jnp.eye(2 * BW, dtype=generator.dtype) + jnp.concatenate([upper_half, lower_half], 0)
    for sweep in range(NS_STEPS):
        product = lax.dot_general(iterate, iterate, ROWS_DIM, precision=lax.Precision.HIGHEST)
        iterate = 1.5 * iterate - 0.5 * jnp.dot(iterate, product, precision=lax.Precision.HIGHEST)
    return iterate


def statistics(blocks):
    cross_part = lax.dot_general(
        blocks[:, :BW], blocks[:, BW:], ROWS_DIM, precision=lax.Precision.HIGHEST
    )
    square_part = jnp.sum(blocks * blocks, axis=0)
    return lax.psum((cross_part, square_part), "rows")


def assemble(first, incoming, staying):
    return jnp.where(
        first, jnp.concatenate([incoming, staying], -1), jnp.concatenate([staying, incoming], -1)
    )


def general_body(snapshots, grades, mover):
    blocks = snapshots
    labels = grades.astype(jnp.float32)
    for round_index in range(ROUNDS):
        cross_gram, squares = statistics(blocks)
        rotator = rotation(cross_gram, squares, labels)
        blocks = jnp.dot(blocks, rotator, precision=lax.Precision.HIGHEST)
        if round_index + 1 < ROUNDS:
            first = mover[round_index, 0] == 0
            move_label = jnp.where(first, labels[:BW], labels[BW:])
            stay_label = jnp.where(first, labels[BW:], labels[:BW])
            moving = jnp.where(first, blocks[:, :BW], blocks[:, BW:])
            staying = jnp.where(first, blocks[:, BW:], blocks[:, :BW])
            incoming, came_label = from_behind((moving, move_label), "blk", 1)
            blocks = assemble(first, incoming, staying)
            labels = assemble(first, came_label, stay_label)
    return blocks


def split(value):
    high = value.astype(jnp.bfloat16)
    return high, (value - high.astype(jnp.float32)).astype(jnp.bfloat16)


def dot_split(a, b, dims=PLAIN):
    (ah, al), (bh, bl) = a, b
    mul = functools.partial(lax.dot_general, dimension_numbers=dims, preferred_element_type=jnp.float32)
    return mul(ah, bh) + (mul(ah, bl) + mul(al, bh))


def dot3(a, b, dims=PLAIN):
    return dot_split(split(a), split(b), dims)


def dot6(a, b, dims=PLAIN):
    return lax.dot_general(
        a, b, dims, precision=lax.Precision.HIGHEST, preferred_element_type=jnp.float32
    )


def turn_kernel(
    n, x_hbm, grade_hbm, mover_hbm, held_ref, high_ref, low_ref, last_high, last_low,
    x_ref, near_ref, x_high, x_low, near_high, near_low, grade_ref, mover_ref, meta_ref, meta,
    dpart, dgot, dmid, dnear, dall, diag_ref, turn_ref, flip_ref, fac_ref,
    cpart, cgot, cmid, cnear, cmine, cother, cfull,
    x_send, x_recv, rs_send, rs_recv, ag_send, ag_recv, sib_send, sib_recv, one_send, one_recv,
    pass_send, pass_recv, load_sem, side_sem, ready_sem,
):
    pos, me = lax.axis_index("blk"), lax.axis_index("rows")
    other = 1 - pos
    core, group = lax.rem(me, 2), me // 2
    groups = n // 2
    rows, width = x_ref.shape
    half = rows // 2
    piece = half // CHUNKS
    share = width // n
    partner, sibling = (other, me), (pos, me + 1 - 2 * core)
    peers = [None] + [lax.rem(group + k, groups) for k in range(1, groups)]

    barrier = pltpu.get_barrier_semaphore()
    for device in ((other, me - core), sibling):
        pl.semaphore_signal(barrier, inc=1, device_id=device, device_id_type=MESH)
    for peer in peers[1:]:
        pl.semaphore_signal(barrier, inc=1, device_id=(pos, 2 * peer + 1), device_id_type=MESH)
    loads = []
    for i in range(LOADS):
        part = pl.ds(i * (rows // LOADS), rows // LOADS)
        loads.append(pltpu.make_async_copy(x_hbm.at[part], x_ref.at[part], load_sem.at[i]))
    sides = [
        pltpu.make_async_copy(grade_hbm, grade_ref, side_sem.at[0]),
        pltpu.make_async_copy(mover_hbm, mover_ref, side_sem.at[1]),
    ]
    for copy in sides + loads:
        copy.start()

    def relay(source):
        @pl.when(core == source)
        def _():
            pl.semaphore_signal(ready_sem, inc=1, device_id=sibling, device_id_type=MESH)

        @pl.when(core != source)
        def _():
            pl.semaphore_wait(ready_sem, 1)

    @pl.when(core == 0)
    def _():
        pl.semaphore_wait(barrier, 3)

    relay(0)

    def remote(src, dst, send, recv, device):
        copy = pltpu.make_async_remote_copy(
            src_ref=src, dst_ref=dst, send_sem=send, recv_sem=recv,
            device_id=device, device_id_type=MESH,
        )
        copy.start()
        return copy

    swaps = []
    for c in range(2 * CHUNKS):
        start = lax.rem(other * half + c * piece, rows)
        swaps.append(
            pltpu.make_async_remote_copy(
                src_ref=(x_hbm if c < DIRECT else x_ref).at[pl.ds(pl.multiple_of(start, piece), piece)],
                dst_ref=near_ref.at[pl.ds(c * piece, piece)],
                send_sem=x_send.at[c], recv_sem=x_recv.at[c],
                device_id=partner, device_id_type=MESH,
            )
        )

    def send(first, last):
        for c in range(first, last):
            swaps[c].start()

    send(0, DIRECT)
    for copy in loads:
        copy.wait()
    send(DIRECT, FIRST)
    for copy in sides:
        copy.wait()
    meta[...] = jnp.zeros_like(meta)
    meta[0:1, :] = grade_ref[...].astype(jnp.float32)
    for r in range(ROUNDS - 1):
        meta[r + 1:r + 2, :] = jnp.full((1, width), mover_ref[r], jnp.int32).astype(jnp.float32)
    meta_ref[pos] = meta[...]
    labels = remote(meta, meta_ref.at[pos], one_send.at[0], one_recv.at[0], partner)

    def pair_up(part, got, which):
        return remote(part.at[1 - core], got, sib_send.at[which], sib_recv.at[which], sibling)

    def scatter(mid, near, which):
        return [
            remote(
                mid.at[peers[k]], near.at[k], rs_send.at[which, k], rs_recv.at[which, k],
                (pos, 2 * peers[k] + core),
            )
            for k in range(1, groups)
        ]

    def rotated(pair, p):
        return split(dot_split(pair, (turn_ref[p, 0], turn_ref[p, 1])))

    def summed(mid, near, copies):
        total = mid[group]
        for k in range(1, groups):
            copies[k - 1].wait()
            total = total + near[k]
        return total

    def gather(full, which):
        return [
            remote(
                full.at[core, group], full.at[core, group], ag_send.at[which, k],
                ag_recv.at[which, k], (pos, 2 * peers[k] + core),
            )
            for k in range(1, groups)
        ]

    def hand_over(full, copies, which):
        for copy in copies:
            copy.wait()
        return remote(full.at[core], full.at[core], sib_send.at[which], sib_recv.at[which], sibling)

    def receive(c):
        swaps[c].wait()
        there = slice(c * piece, (c + 1) * piece)
        near_high[there, :], near_low[there, :] = split(near_ref[there, :])

    def cross(c):
        receive(c)
        here = pl.ds(pl.multiple_of(pos * half + c * piece, piece), piece)
        there = slice(c * piece, (c + 1) * piece)
        mine = x_high[here, :], x_low[here, :]
        theirs = near_high[there, :], near_low[there, :]
        left = [jnp.where(pos == 0, a, b) for a, b in zip(mine, theirs)]
        right = [jnp.where(pos == 0, b, a) for a, b in zip(mine, theirs)]
        return dot_split(left, right, ROWS_DIM)

    both = jnp.zeros((width, 2 * width), jnp.float32)
    for i in range(LOADS):
        part = slice(i * (rows // LOADS), (i + 1) * (rows // LOADS))
        high, low = split(x_ref[part, :])
        x_high[part, :] = high
        x_low[part, :] = low
        both = both + lax.dot_general(
            high, jnp.concatenate([high, low], 1), ROWS_DIM, preferred_element_type=jnp.float32
        )
    own = both[:, :width] + (both[:, width:] + both[:, width:].T)
    dpart[...] = own.reshape(2, groups, share, width)
    copy = pair_up(dpart, dgot, 0)
    copy.wait()
    dmid[...] = dpart[core] + dgot[...]

    @pl.when(core == 1)
    def _():
        pl.semaphore_wait(barrier, 2 * groups - 1)

    relay(1)
    copies = scatter(dmid, dnear, 0)
    total = cross(0)
    dall[pos, core, group] = summed(dmid, dnear, copies)
    mine, theirs = dall.at[pos], dall.at[other]
    here = mine.at[core, group]
    d_swap = remote(here, here, one_send.at[1], one_recv.at[1], partner)
    own_copies = gather(mine, 0)
    send(FIRST, CHUNKS + SOON)
    total = total + cross(1)
    d_swap.wait()
    their_copies = gather(theirs, 1)
    own_copy = hand_over(mine, own_copies, 1)
    total = total + cross(2)

    def begin_round(p, work=()):
        begin(p, dall[p].reshape(width, width), meta_ref, turn_ref, flip_ref, diag_ref, work)

    own_copy.wait()
    handed = []

    def pass_on():
        handed.append(hand_over(theirs, their_copies, 2))

    begin_round(pos, [lambda: None, lambda: None, pass_on])
    total = total + cross(3)
    labels.wait()
    handed[0].wait()
    begin_round(other)
    for c in range(4, CHUNKS - 1):
        total = total + cross(c)
    last = CHUNKS - 1
    here = pl.ds(pl.multiple_of(pos * half + last * piece, piece), piece)
    mine = rotated((x_high[here, :], x_low[here, :]), pos)
    left = flip_ref[0, 0], flip_ref[0, 1]
    right = turn_ref[1, 0], turn_ref[1, 1]
    total = dot_split(left, split(dot_split(split(total), right)))
    receive(last)
    there = slice(last * piece, (last + 1) * piece)
    theirs = rotated((near_high[there, :], near_low[there, :]), other)
    left = [jnp.where(pos == 0, a, b) for a, b in zip(mine, theirs)]
    right = [jnp.where(pos == 0, b, a) for a, b in zip(mine, theirs)]
    total = total + dot_split(left, right, ROWS_DIM)
    cpart[...] = total.reshape(2, groups, share, width)
    copy = pair_up(cpart, cgot, 3)
    copy.wait()
    cmid[...] = cpart[core] + cgot[...]
    copies = scatter(cmid, cnear, 1)
    prepare(pos, meta_ref, diag_ref, fac_ref)
    cmine[...] = summed(cmid, cnear, copies)
    c_swap = remote(cmine, cother, one_send.at[2], one_recv.at[2], partner)
    send(CHUNKS + SOON, 2 * CHUNKS)
    c_swap.wait()
    cfull[core, group] = cmine[...] + cother[...]
    copies = gather(cfull, 2)
    passed = []
    for k in range(groups):
        if k > 0:
            copies[k - 1].wait()
        held = cfull.at[core, lax.rem(group + groups - k, groups)]
        passed.append(remote(held, held, pass_send.at[k], pass_recv.at[k], sibling))
    for copy in passed:
        copy.wait()
    chain(
        pos, cfull[...].reshape(width, width), diag_ref, turn_ref, flip_ref, meta_ref, fac_ref,
        high_ref, low_ref,
    )
    tile = TALL * piece
    for t in range(rows // tile):
        for c in range(max(t * TALL, CHUNKS), (t + 1) * TALL):
            receive(c)
        here = pl.ds(pl.multiple_of(lax.rem(pos * half + t * tile, rows), tile), tile)
        there = slice(t * tile, (t + 1) * tile)
        high = jnp.concatenate([x_high[here, :], near_high[there, :]], 1)
        low = jnp.concatenate([x_low[here, :], near_low[there, :]], 1)
        late = t - (rows // tile - AFTER)
        if late < 0:
            held_ref[there, :] = dot_split((high, low), (high_ref[...], low_ref[...]))
        else:
            after = slice(late * tile, (late + 1) * tile)
            last_high[after, :] = high
            last_low[after, :] = low


def eye(n):
    return (
        lax.broadcasted_iota(jnp.int32, (n, n), 0) == lax.broadcasted_iota(jnp.int32, (n, n), 1)
    ).astype(jnp.float32)


def cut3(value):
    high, rest = value.astype(jnp.bfloat16), None
    rest = value - high.astype(jnp.float32)
    middle = rest.astype(jnp.bfloat16)
    return high, middle, (rest - middle.astype(jnp.float32)).astype(jnp.bfloat16)


def mul(a, b, dims=PLAIN):
    return lax.dot_general(a, b, dims, preferred_element_type=jnp.float32)


def fine_left(a, b):
    (ah, am, al), (bh, bl) = a, b
    return mul(ah, bh) + ((mul(ah, bl) + mul(am, bh)) + (mul(am, bl) + mul(al, bh)))


def fine_right(a, b):
    (ah, al), (bh, bm, bl) = a, b
    return mul(ah, bh) + ((mul(ah, bm) + mul(al, bh)) + (mul(al, bm) + mul(ah, bl)))


def rotate(crosses, signs, work=()):
    work = list(work)
    unit = eye(BW)
    both = range(2)
    each = range(len(crosses))
    total = [jnp.sum(h * h, keepdims=True) + epsilon for h in crosses]
    cut = [split(h) for h in crosses]
    flip = [split(h.T) for h in crosses]
    scale = [relaxation * relaxation / t for t in total]
    m = [[scale[i] * dot_split(cut[i], flip[i]), scale[i] * dot_split(flip[i], cut[i])] for i in each]
    b = [relaxation * lax.rsqrt(total[i]) * signs[i] * crosses[i] for i in each]
    bc = [split(v) for v in b]
    if work:
        work.pop(0)()
    mc = [[split(v) for v in pair] for pair in m]
    m2 = [[dot_split(v, v) for v in pair] for pair in mc]
    mb = [dot_split(mc[i][0], bc[i]) for i in each]
    if work:
        work.pop(0)()
    m2c = [[split(v) for v in pair] for pair in m2]
    m3 = [[dot_split(m2c[i][j], mc[i][j]) for j in both] for i in each]
    m4 = [[dot_split(v, v) for v in pair] for pair in m2c]
    m2b = [dot_split(m2c[i][0], bc[i]) for i in each]
    m3b = [dot_split(m2c[i][0], split(mb[i])) for i in each]
    if work:
        work.pop(0)()
    n = [[0.75 * m2[i][j] - 0.25 * m3[i][j] for j in both] for i in each]
    p = [
        [
            unit - 0.5 * m[i][j] + 0.375 * m2[i][j] - 0.3125 * m3[i][j] + 0.0625 * m4[i][j]
            for j in both
        ]
        for i in each
    ]
    nb = [split(0.75 * m2b[i] - 0.25 * m3b[i]) for i in each]
    nc = [[split(v) for v in pair] for pair in n]
    pc = [[split(v) for v in pair] for pair in p]
    u = [[split(dot_split(v, v)) for v in pair] for pair in nc]
    r = [[split(dot_split(pc[i][j], split(0.375 * unit + 0.125 * n[i][j]))) for j in both] for i in each]
    pb = [dot_split(pc[i][0], bc[i]) for i in each]
    nnb = [split(dot_split(nc[i][0], nb[i])) for i in each]
    if work:
        work.pop(0)()
    out = []
    for i in each:
        gain = [p[i][j] + dot_split(r[i][j], u[i][j]) for j in both]
        out.append((gain[0], pb[i] + dot_split(r[i][0], nnb[i]), gain[1]))
    for step in work:
        step()
    return out


def columns(q):
    upper, edge, lower = q
    return (
        split(jnp.concatenate([upper, -edge.T], 0)), split(jnp.concatenate([edge, lower], 0))
    )


def turned(q):
    upper, edge, lower = q
    return (
        split(jnp.concatenate([upper, -edge], 1)), split(jnp.concatenate([edge.T, lower], 1))
    )


def choose(flag, a, b):
    return tuple(jnp.where(flag, u, v) for u, v in zip(a, b))


def order(flag, pair):
    return choose(flag, pair[1], pair[0]), choose(flag, pair[0], pair[1])


def beside(a, b, axis=1):
    return tuple(jnp.concatenate([u, v], axis) for u, v in zip(a, b))


def plan(meta_ref):
    flags, signs, kept = [], [], [1.0, 1.0]
    labels = [[meta_ref[p, 0:1, :BW], meta_ref[p, 0:1, BW:]] for p in range(2)]
    names = []
    for r in range(ROUNDS - 1):
        first = [1.0 - meta_ref[p, r + 1:r + 2, :BW] for p in range(2)]
        flag = [jnp.abs(first[p] - kept[p]) < 0.5 for p in range(2)]
        kept = [1.0 - first[0], first[1]]
        labels = [
            [jnp.where(flag[p], labels[p][1], labels[p][0]), jnp.where(flag[p], labels[p][0], labels[p][1])]
            for p in range(2)
        ]
        labels = [[labels[0][0], labels[1][1]], [labels[0][1], labels[1][0]]]
        flags.append(flag)
        signs.append([2.0 * k - 1.0 for k in kept])
        names.append(labels)
    return flags, signs, names


def tall(row):
    return jnp.broadcast_to(row, (BW, BW)).T


def weight(pair):
    return 1.0 / (1.0 + jnp.abs(tall(pair[0]) - pair[1]))


def begin(p, diag, meta_ref, turn_ref, flip_ref, diag_ref, work=()):
    unit = eye(BW)
    labels = meta_ref[p, 0:1, :]
    left = jnp.sum(diag[:BW, :BW] * unit, axis=1, keepdims=True)
    right = jnp.sum(diag[BW:, BW:] * unit, axis=0, keepdims=True)
    scale = lax.rsqrt(left + epsilon) * lax.rsqrt(right + epsilon)
    cross = diag[:BW, BW:] * (scale * weight((labels[:, :BW], labels[:, BW:])))
    (q,) = rotate([cross], [1.0], work)
    flag = meta_ref[p, 1:2, :BW] < 0.5
    q_cut = beside(*order(flag, columns(q)))
    wide = jnp.concatenate([flag, flag], 1)
    flip = beside(*order(wide, turned(q)), 0)
    for k in range(2):
        turn_ref[p, k] = q_cut[k]
        flip_ref[p, k] = flip[k]
    diag_ref[p] = fine_right(flip, cut3(fine_left(cut3(diag), q_cut)))


def prepare(pos, meta_ref, diag_ref, fac_ref):
    unit = eye(BW)
    flags, signs, names = plan(meta_ref)

    def scales(p, s, axis):
        part = slice(s * BW, s * BW + BW)
        return lax.rsqrt(jnp.sum(diag_ref[p, part, part] * unit, axis=axis, keepdims=True) + epsilon)

    fac_ref[0] = weight(names[0][0]) * scales(0, 0, 1) * scales(1, 1, 0)
    fac_ref[1] = weight(names[0][1]) * scales(0, 1, 1) * scales(1, 0, 0)
    fac_ref[2] = weight(names[1][0])
    fac_ref[3] = weight(names[1][1])
    fac_ref[4] = weight([jnp.where(pos == 0, a, b) for a, b in zip(*names[2])])


def chain(pos, between, diag_ref, turn_ref, flip_ref, meta_ref, fac_ref, high_ref, low_ref):
    assert ROUNDS == 4
    flags, signs, _ = plan(meta_ref)
    low, top = slice(0, BW), slice(BW, 2 * BW)
    turn = [(turn_ref[p, 0], turn_ref[p, 1]) for p in range(2)]

    def part(pair, rows=slice(None), cols=slice(None)):
        return tuple(v[rows, cols] for v in pair)

    held = {}
    x0, x1 = between[low, top], between[top, low]
    held["stay"], held["move"] = between[low, low], between[top, top]
    qs = rotate([x0 * fac_ref[0], x1 * fac_ref[1]], signs[0])
    d0 = jnp.concatenate([
        jnp.concatenate([diag_ref[0, low, low], x0], 1),
        jnp.concatenate([x0.T, diag_ref[1, top, top]], 1),
    ], 0)
    d1 = jnp.concatenate([
        jnp.concatenate([diag_ref[0, top, top], x1], 1),
        jnp.concatenate([x1.T, diag_ref[1, low, low]], 1),
    ], 0)
    g = jnp.concatenate([
        jnp.concatenate([diag_ref[0, low, top], held["stay"]], 1),
        jnp.concatenate([held["move"].T, diag_ref[1, top, low]], 1),
    ], 0)
    small = eye(2 * BW)
    row0 = jnp.sum(d0 * small, axis=0, keepdims=True)
    tall1 = jnp.sum(d1 * small, axis=1, keepdims=True)
    d0, d1, g = split(d0 - row0 * small), split(d1 - tall1 * small), split(g)
    q = [beside(*order(flags[1][p], columns(qs[p]))) for p in range(2)]
    wide = [jnp.concatenate([flags[1][p]] * 2, 1) for p in range(2)]
    qt = [beside(*order(wide[p], turned(qs[p])), 0) for p in range(2)]

    def full(pair):
        return pair[0].astype(jnp.float32) + pair[1].astype(jnp.float32)

    mid = split(dot_split(g, q[1]))
    t0 = full(qt[0]) * row0 + dot_split(qt[0], d0)
    t1 = full(q[1]) * tall1 + dot_split(d1, q[1])
    x0 = dot_split(part(qt[0], low), part(mid, cols=top))
    x1 = dot_split(part(qt[0], top), part(mid, cols=low))

    sq0 = lax.rsqrt(jnp.sum(full(qt[0]) * t0, axis=1, keepdims=True) + epsilon)
    sq1 = lax.rsqrt(jnp.sum(full(q[1]) * t1, axis=0, keepdims=True) + epsilon)

    def rest0():
        held["stay"] = dot_split(part(qt[0], low), part(mid, cols=low))
        held["move"] = dot_split(part(qt[0], top), part(mid, cols=top))
        held["d0"] = fine_left(cut3(t0), q[0])

    def rest1():
        held["d1"] = fine_right(qt[1], cut3(t1))
        held["w00"] = dot_split(part(turn[0], cols=low), part(q[0], low))

    def rest2():
        held["w01"] = dot_split(part(turn[1], cols=top), part(q[0], top))
        held["w10"] = dot_split(part(turn[0], cols=top), part(q[1], low))

    def rest3():
        held["w11"] = dot_split(part(turn[1], cols=low), part(q[1], top))

    qs = rotate(
        [x0 * (fac_ref[2] * sq0[low] * sq1[:, top]), x1 * (fac_ref[3] * sq0[top] * sq1[:, low])],
        signs[1], [rest0, rest1, rest2, rest3],
    )
    e0, e1 = held["d0"], held["d1"]
    d0 = split(jnp.concatenate([
        jnp.concatenate([e0[low, low], x0], 1), jnp.concatenate([x0.T, e1[top, top]], 1),
    ], 0))
    d1 = split(jnp.concatenate([
        jnp.concatenate([e0[top, top], x1], 1), jnp.concatenate([x1.T, e1[low, low]], 1),
    ], 0))
    g = split(jnp.concatenate([
        jnp.concatenate([e0[low, top], held["stay"]], 1),
        jnp.concatenate([held["move"].T, e1[top, low]], 1),
    ], 0))
    mine = pos == 0
    wide = jnp.concatenate([flags[2][0]] * 2, 1)
    stay, move = order(wide, turned(qs[0]))
    up = choose(mine, stay, move)
    stay, move = order(flags[2][0], columns(qs[0]))
    upright = choose(mine, stay, move)
    stay, move = order(flags[2][1], columns(qs[1]))
    side = choose(mine, move, stay)
    mid = split(dot_split(g, side))
    t0 = dot_split(up, d0)
    t1 = dot_split(d1, side)
    x = dot_split(up, mid)
    sq0 = lax.rsqrt(jnp.sum(full(up) * t0, axis=1, keepdims=True) + epsilon)
    sq1 = lax.rsqrt(jnp.sum(full(side) * t1, axis=0, keepdims=True) + epsilon)
    rows = [None, None]

    def tail(r):
        def run():
            a, b = held["w0" + str(r)], held["w1" + str(r)]
            first = split(jnp.concatenate([a[:, low], b[:, top]], 1))
            second = split(jnp.concatenate([a[:, top], b[:, low]], 1))
            rows[r] = split(jnp.concatenate([dot_split(first, upright), dot_split(second, side)], 1))
        return run

    sign = jnp.where(mine, signs[2][0], signs[2][1])
    (last,) = rotate([x * (fac_ref[4] * sq0 * sq1)], [sign], [tail(0), tail(1)])
    a, b = columns(last)
    last = beside(choose(sign > 0.0, a, b), choose(sign > 0.0, b, a))
    out = [split(dot_split(rows[r], last)) for r in range(2)]
    width = 2 * BW
    for p in range(2):
        high, lower = choose(mine, out[p], out[1 - p])
        high_ref[p * width:(p + 1) * width] = high
        low_ref[p * width:(p + 1) * width] = lower


def write_kernel(tile, held_ref, high_ref, low_ref, last_high, last_low, out_ref, made, sems):
    early, rows = held_ref.shape[0], out_ref.shape[0]
    pos = lax.axis_index("blk")
    copies = []

    def write(t, source):
        there = pl.ds(pl.multiple_of(lax.rem(pos * (rows // 2) + t * tile, rows), tile), tile)
        copies.append(pltpu.make_async_copy(source, out_ref.at[there], sems.at[t]))
        copies[-1].start()

    for t in range(early // tile):
        write(t, held_ref.at[pl.ds(t * tile, tile)])
    for t in range(early // tile, rows // tile):
        here = slice(t * tile - early, (t + 1) * tile - early)
        made[here, :] = dot_split((last_high[here, :], last_low[here, :]), (high_ref[...], low_ref[...]))
        write(t, made.at[pl.ds(t * tile - early, tile)])
    for copy in copies:
        copy.wait()


def pair_body(n, snapshots, grades, mover):
    rows, width = snapshots.shape
    share = width // n
    f32 = jnp.float32
    dma = pltpu.SemaphoreType.DMA
    whole = pltpu.VMEM((2, n // 2, share, width), f32)
    part = pltpu.VMEM((n // 2, share, width), f32)
    one = pltpu.VMEM((share, width), f32)
    everything = pltpu.VMEM((rows, width), f32)
    cut = pltpu.VMEM((rows, width), jnp.bfloat16)
    square = pltpu.VMEM((2, width, width), f32)
    turn = pltpu.VMEM((2, 2, width, width), jnp.bfloat16)
    operands = [
        pltpu.with_memory_space_constraint(value, pltpu.HBM)
        for value in (snapshots, grades.reshape(1, width), mover.reshape(ROUNDS - 1))
    ]
    tile = TALL * (rows // 2 // CHUNKS)
    late = AFTER * tile
    bf16 = jnp.bfloat16
    made = pl.pallas_call(
        functools.partial(turn_kernel, n),
        out_shape=(
            jax.ShapeDtypeStruct((rows - late, width), f32),
            jax.ShapeDtypeStruct((2 * width, width), bf16),
            jax.ShapeDtypeStruct((2 * width, width), bf16),
            jax.ShapeDtypeStruct((late, 2 * width), bf16),
            jax.ShapeDtypeStruct((late, 2 * width), bf16),
        ),
        in_specs=[HBM] * 3,
        out_specs=(VMEM,) * 5,
        scratch_shapes=[
            everything, everything, cut, cut, cut, cut, pltpu.VMEM((1, width), jnp.int32),
            pltpu.SMEM((ROUNDS - 1,), jnp.int32),
            pltpu.VMEM((2, 8, width), f32), pltpu.VMEM((8, width), f32),
            whole, part, part, part, pltpu.VMEM((2, 2, n // 2, share, width), f32), square, turn, turn,
            pltpu.VMEM((5, BW, BW), f32),
            whole, part, part, part, one, one, whole,
            dma((2 * CHUNKS,)), dma((2 * CHUNKS,)),
            dma((2, n // 2)), dma((2, n // 2)), dma((3, n // 2)), dma((3, n // 2)),
            dma((4,)), dma((4,)), dma((3,)), dma((3,)), dma((n // 2,)), dma((n // 2,)),
            dma((LOADS,)), dma((2,)), pltpu.SemaphoreType.REGULAR,
        ],
        compiler_params=pltpu.CompilerParams(
            collective_id=0, has_side_effects=True, vmem_limit_bytes=40 * 1024 * 1024
        ),
    )(*operands)
    return pl.pallas_call(
        functools.partial(write_kernel, tile),
        out_shape=jax.ShapeDtypeStruct((rows, width), f32),
        in_specs=[VMEM] * 5,
        out_specs=ANY,
        scratch_shapes=[pltpu.VMEM((late, width), f32), dma((rows // tile,))],
        compiler_params=pltpu.CompilerParams(vmem_limit_bytes=8 * 1024 * 1024),
    )(*made)


def solution(mesh):
    placed = (P("rows", "blk"), P("blk"), P(None, "blk"))
    n = mesh.shape["rows"]
    pairs = mesh.shape["blk"] == 2 and n % 2 == 0 and (2 * BW) % (8 * n) == 0
    body = functools.partial(pair_body, n) if pairs else general_body
    return jax.shard_map(
        body, mesh=mesh, in_specs=placed, out_specs=P("rows", "blk"), check_vma=False
    )
```

```python
import functools

import jax
import jax.numpy as jnp
from jax import lax
from jax.experimental import pallas as pl
from jax.experimental.pallas import tpu as pltpu
from jax.sharding import PartitionSpec as P

BW = 128
ROUNDS = 4
NS_STEPS = 3
CHUNKS = 8
FIRST = 3
DIRECT = 1
SOON = 3
AHEAD = 4
TALL = 2
LOADS = 4

epsilon = 1e-06
relaxation = 1.2

MESH = pl.DeviceIdType.MESH
ROWS_DIM = (((0,), (0,)), ((), ()))
PLAIN = (((1,), (0,)), ((), ()))
VMEM = pl.BlockSpec(memory_space=pltpu.VMEM)
ANY = pl.BlockSpec(memory_space=pl.ANY)
HBM = pl.BlockSpec(memory_space=pltpu.HBM)


def from_behind(value, axis, by):
    peers = lax.axis_size(axis)
    return lax.ppermute(value, axis, [(i, (i + by) % peers) for i in range(peers)])


def rotation(cross_gram, squares, labels):
    left_scale = lax.rsqrt(squares[:BW] + epsilon)
    right_scale = lax.rsqrt(squares[BW:] + epsilon)
    grade_gap = jnp.abs(labels[:BW, None] - labels[None, BW:])
    scaled = cross_gram * left_scale[:, None] * right_scale[None, :] / (1.0 + grade_gap)
    magnitude = jnp.sqrt(jnp.sum(scaled * scaled) + epsilon)
    generator = relaxation * scaled / magnitude
    zeros_block = jnp.zeros_like(generator)
    upper_half = jnp.concatenate([zeros_block, generator], 1)
    lower_half = jnp.concatenate([-generator.T, zeros_block], 1)
    iterate = jnp.eye(2 * BW, dtype=generator.dtype) + jnp.concatenate([upper_half, lower_half], 0)
    for sweep in range(NS_STEPS):
        product = lax.dot_general(iterate, iterate, ROWS_DIM, precision=lax.Precision.HIGHEST)
        iterate = 1.5 * iterate - 0.5 * jnp.dot(iterate, product, precision=lax.Precision.HIGHEST)
    return iterate


def statistics(blocks):
    cross_part = lax.dot_general(
        blocks[:, :BW], blocks[:, BW:], ROWS_DIM, precision=lax.Precision.HIGHEST
    )
    square_part = jnp.sum(blocks * blocks, axis=0)
    return lax.psum((cross_part, square_part), "rows")


def assemble(first, incoming, staying):
    return jnp.where(
        first, jnp.concatenate([incoming, staying], -1), jnp.concatenate([staying, incoming], -1)
    )


def general_body(snapshots, grades, mover):
    blocks = snapshots
    labels = grades.astype(jnp.float32)
    for round_index in range(ROUNDS):
        cross_gram, squares = statistics(blocks)
        rotator = rotation(cross_gram, squares, labels)
        blocks = jnp.dot(blocks, rotator, precision=lax.Precision.HIGHEST)
        if round_index + 1 < ROUNDS:
            first = mover[round_index, 0] == 0
            move_label = jnp.where(first, labels[:BW], labels[BW:])
            stay_label = jnp.where(first, labels[BW:], labels[:BW])
            moving = jnp.where(first, blocks[:, :BW], blocks[:, BW:])
            staying = jnp.where(first, blocks[:, BW:], blocks[:, :BW])
            incoming, came_label = from_behind((moving, move_label), "blk", 1)
            blocks = assemble(first, incoming, staying)
            labels = assemble(first, came_label, stay_label)
    return blocks


def split(value):
    high = value.astype(jnp.bfloat16)
    return high, (value - high.astype(jnp.float32)).astype(jnp.bfloat16)


def dot_split(a, b, dims=PLAIN):
    (ah, al), (bh, bl) = a, b
    mul = functools.partial(lax.dot_general, dimension_numbers=dims, preferred_element_type=jnp.float32)
    return mul(ah, bh) + (mul(ah, bl) + mul(al, bh))


def dot3(a, b, dims=PLAIN):
    return dot_split(split(a), split(b), dims)


def dot6(a, b, dims=PLAIN):
    return lax.dot_general(
        a, b, dims, precision=lax.Precision.HIGHEST, preferred_element_type=jnp.float32
    )


def turn_kernel(
    n, x_hbm, grade_hbm, mover_hbm, held_ref, high_ref, low_ref, last_high, last_low,
    x_ref, near_ref, x_high, x_low, near_high, near_low, grade_ref, mover_ref, meta_ref, meta,
    dpart, dgot, dmid, dnear, dall, diag_ref, turn_ref, flip_ref, fac_ref,
    cpart, cgot, cmid, cnear, cmine, cother, cfull,
    x_send, x_recv, rs_send, rs_recv, ag_send, ag_recv, sib_send, sib_recv, one_send, one_recv,
    pass_send, pass_recv, load_sem, side_sem, ready_sem,
):
    pos, me = lax.axis_index("blk"), lax.axis_index("rows")
    other = 1 - pos
    core, group = lax.rem(me, 2), me // 2
    groups = n // 2
    rows, width = x_ref.shape
    half = rows // 2
    piece = half // CHUNKS
    share = width // n
    partner, sibling = (other, me), (pos, me + 1 - 2 * core)
    peers = [None] + [lax.rem(group + k, groups) for k in range(1, groups)]

    barrier = pltpu.get_barrier_semaphore()
    for device in ((other, me - core), sibling):
        pl.semaphore_signal(barrier, inc=1, device_id=device, device_id_type=MESH)
    for peer in peers[1:]:
        pl.semaphore_signal(barrier, inc=1, device_id=(pos, 2 * peer + 1), device_id_type=MESH)
    loads = []
    for i in range(LOADS):
        part = pl.ds(i * (rows // LOADS), rows // LOADS)
        loads.append(pltpu.make_async_copy(x_hbm.at[part], x_ref.at[part], load_sem.at[i]))
    sides = [
        pltpu.make_async_copy(grade_hbm, grade_ref, side_sem.at[0]),
        pltpu.make_async_copy(mover_hbm, mover_ref, side_sem.at[1]),
    ]
    for copy in sides + loads:
        copy.start()

    def relay(source):
        @pl.when(core == source)
        def _():
            pl.semaphore_signal(ready_sem, inc=1, device_id=sibling, device_id_type=MESH)

        @pl.when(core != source)
        def _():
            pl.semaphore_wait(ready_sem, 1)

    @pl.when(core == 0)
    def _():
        pl.semaphore_wait(barrier, 3)

    relay(0)

    def remote(src, dst, send, recv, device):
        copy = pltpu.make_async_remote_copy(
            src_ref=src, dst_ref=dst, send_sem=send, recv_sem=recv,
            device_id=device, device_id_type=MESH,
        )
        copy.start()
        return copy

    swaps = []
    for c in range(2 * CHUNKS):
        start = lax.rem(other * half + c * piece, rows)
        swaps.append(
            pltpu.make_async_remote_copy(
                src_ref=(x_hbm if c < DIRECT else x_ref).at[pl.ds(pl.multiple_of(start, piece), piece)],
                dst_ref=near_ref.at[pl.ds(c * piece, piece)],
                send_sem=x_send.at[c], recv_sem=x_recv.at[c],
                device_id=partner, device_id_type=MESH,
            )
        )

    def send(first, last):
        for c in range(first, last):
            swaps[c].start()

    send(0, DIRECT)
    for copy in loads:
        copy.wait()
    send(DIRECT, FIRST)
    for copy in sides:
        copy.wait()
    meta[...] = jnp.zeros_like(meta)
    meta[0:1, :] = grade_ref[...].astype(jnp.float32)
    for r in range(ROUNDS - 1):
        meta[r + 1:r + 2, :] = jnp.full((1, width), mover_ref[r], jnp.int32).astype(jnp.float32)
    meta_ref[pos] = meta[...]
    labels = remote(meta, meta_ref.at[pos], one_send.at[0], one_recv.at[0], partner)

    def pair_up(part, got, which):
        return remote(part.at[1 - core], got, sib_send.at[which], sib_recv.at[which], sibling)

    def scatter(mid, near, which):
        return [
            remote(
                mid.at[peers[k]], near.at[k], rs_send.at[which, k], rs_recv.at[which, k],
                (pos, 2 * peers[k] + core),
            )
            for k in range(1, groups)
        ]

    def rotated(pair, p):
        return split(dot_split(pair, (turn_ref[p, 0], turn_ref[p, 1])))

    def summed(mid, near, copies):
        total = mid[group]
        for k in range(1, groups):
            copies[k - 1].wait()
            total = total + near[k]
        return total

    def gather(full, which):
        return [
            remote(
                full.at[core, group], full.at[core, group], ag_send.at[which, k],
                ag_recv.at[which, k], (pos, 2 * peers[k] + core),
            )
            for k in range(1, groups)
        ]

    def hand_over(full, copies, which):
        for copy in copies:
            copy.wait()
        return remote(full.at[core], full.at[core], sib_send.at[which], sib_recv.at[which], sibling)

    def receive(c):
        swaps[c].wait()
        there = slice(c * piece, (c + 1) * piece)
        near_high[there, :], near_low[there, :] = split(near_ref[there, :])

    def cross(c):
        receive(c)
        here = pl.ds(pl.multiple_of(pos * half + c * piece, piece), piece)
        there = slice(c * piece, (c + 1) * piece)
        mine = x_high[here, :], x_low[here, :]
        theirs = near_high[there, :], near_low[there, :]
        left = [jnp.where(pos == 0, a, b) for a, b in zip(mine, theirs)]
        right = [jnp.where(pos == 0, b, a) for a, b in zip(mine, theirs)]
        return dot_split(left, right, ROWS_DIM)

    both = jnp.zeros((width, 2 * width), jnp.float32)
    for i in range(LOADS):
        part = slice(i * (rows // LOADS), (i + 1) * (rows // LOADS))
        high, low = split(x_ref[part, :])
        x_high[part, :] = high
        x_low[part, :] = low
        both = both + lax.dot_general(
            high, jnp.concatenate([high, low], 1), ROWS_DIM, preferred_element_type=jnp.float32
        )
    own = both[:, :width] + (both[:, width:] + both[:, width:].T)
    dpart[...] = own.reshape(2, groups, share, width)
    copy = pair_up(dpart, dgot, 0)
    copy.wait()
    dmid[...] = dpart[core] + dgot[...]

    @pl.when(core == 1)
    def _():
        pl.semaphore_wait(barrier, 2 * groups - 1)

    relay(1)
    copies = scatter(dmid, dnear, 0)
    total = cross(0)
    dall[pos, core, group] = summed(dmid, dnear, copies)
    mine, theirs = dall.at[pos], dall.at[other]
    here = mine.at[core, group]
    d_swap = remote(here, here, one_send.at[1], one_recv.at[1], partner)
    own_copies = gather(mine, 0)
    send(FIRST, CHUNKS + SOON)
    ahead = group < groups // AHEAD
    pl.when(ahead)(swaps[CHUNKS + SOON].start)
    total = total + cross(1)
    d_swap.wait()
    their_copies = gather(theirs, 1)
    own_copy = hand_over(mine, own_copies, 1)
    total = total + cross(2)

    def begin_round(p, work=()):
        begin(p, dall[p].reshape(width, width), meta_ref, turn_ref, flip_ref, diag_ref, work)

    own_copy.wait()
    handed = []

    def pass_on():
        handed.append(hand_over(theirs, their_copies, 2))

    begin_round(pos, [lambda: None, lambda: None, pass_on])
    total = total + cross(3)
    labels.wait()
    handed[0].wait()
    begin_round(other)
    for c in range(4, CHUNKS - 1):
        total = total + cross(c)
    last = CHUNKS - 1
    here = pl.ds(pl.multiple_of(pos * half + last * piece, piece), piece)
    mine = rotated((x_high[here, :], x_low[here, :]), pos)
    left = flip_ref[0, 0], flip_ref[0, 1]
    right = turn_ref[1, 0], turn_ref[1, 1]
    total = dot_split(left, split(dot_split(split(total), right)))
    receive(last)
    there = slice(last * piece, (last + 1) * piece)
    theirs = rotated((near_high[there, :], near_low[there, :]), other)
    left = [jnp.where(pos == 0, a, b) for a, b in zip(mine, theirs)]
    right = [jnp.where(pos == 0, b, a) for a, b in zip(mine, theirs)]
    total = total + dot_split(left, right, ROWS_DIM)
    cpart[...] = total.reshape(2, groups, share, width)
    copy = pair_up(cpart, cgot, 3)
    copy.wait()
    cmid[...] = cpart[core] + cgot[...]
    copies = scatter(cmid, cnear, 1)
    prepare(pos, meta_ref, diag_ref, fac_ref)
    beyond = pl.ds(pl.multiple_of(other * half, half), half)
    last_high[:, :width] = x_high[beyond, :]
    last_low[:, :width] = x_low[beyond, :]

    def settle(c):
        swaps[c].wait()
        inside = slice((c - CHUNKS) * piece, (c - CHUNKS + 1) * piece)
        last_high[inside, width:], last_low[inside, width:] = split(
            near_ref[c * piece:(c + 1) * piece, :]
        )

    cmine[...] = summed(cmid, cnear, copies)
    c_swap = remote(cmine, cother, one_send.at[2], one_recv.at[2], partner)
    pl.when(jnp.logical_not(ahead))(swaps[CHUNKS + SOON].start)
    send(CHUNKS + SOON + 1, 2 * CHUNKS)
    c_swap.wait()
    cfull[core, group] = cmine[...] + cother[...]
    copies = gather(cfull, 2)
    for c in range(CHUNKS, CHUNKS + SOON):
        settle(c)
    passed = []
    for k in range(groups):
        if k > 0:
            copies[k - 1].wait()
        held = cfull.at[core, lax.rem(group + groups - k, groups)]
        passed.append(remote(held, held, pass_send.at[k], pass_recv.at[k], sibling))
    for copy in passed:
        copy.wait()
    chain(
        pos, cfull[...].reshape(width, width), diag_ref, turn_ref, flip_ref, meta_ref, fac_ref,
        high_ref, low_ref,
    )
    tile = TALL * piece
    for t in range(half // tile):
        here = pl.ds(pl.multiple_of(pos * half + t * tile, tile), tile)
        there = slice(t * tile, (t + 1) * tile)
        high = jnp.concatenate([x_high[here, :], near_high[there, :]], 1)
        low = jnp.concatenate([x_low[here, :], near_low[there, :]], 1)
        held_ref[there, :] = dot_split((high, low), (high_ref[...], low_ref[...]))
    for c in range(CHUNKS + SOON, 2 * CHUNKS):
        settle(c)


def eye(n):
    return (
        lax.broadcasted_iota(jnp.int32, (n, n), 0) == lax.broadcasted_iota(jnp.int32, (n, n), 1)
    ).astype(jnp.float32)


def cut3(value):
    high, rest = value.astype(jnp.bfloat16), None
    rest = value - high.astype(jnp.float32)
    middle = rest.astype(jnp.bfloat16)
    return high, middle, (rest - middle.astype(jnp.float32)).astype(jnp.bfloat16)


def mul(a, b, dims=PLAIN):
    return lax.dot_general(a, b, dims, preferred_element_type=jnp.float32)


def fine_left(a, b):
    (ah, am, al), (bh, bl) = a, b
    return mul(ah, bh) + ((mul(ah, bl) + mul(am, bh)) + (mul(am, bl) + mul(al, bh)))


def fine_right(a, b):
    (ah, al), (bh, bm, bl) = a, b
    return mul(ah, bh) + ((mul(ah, bm) + mul(al, bh)) + (mul(al, bm) + mul(ah, bl)))


def rotate(crosses, signs, work=()):
    work = list(work)
    unit = eye(BW)
    both = range(2)
    each = range(len(crosses))
    total = [jnp.sum(h * h, keepdims=True) + epsilon for h in crosses]
    cut = [split(h) for h in crosses]
    flip = [split(h.T) for h in crosses]
    scale = [relaxation * relaxation / t for t in total]
    m = [[scale[i] * dot_split(cut[i], flip[i]), scale[i] * dot_split(flip[i], cut[i])] for i in each]
    b = [relaxation * lax.rsqrt(total[i]) * signs[i] * crosses[i] for i in each]
    bc = [split(v) for v in b]
    if work:
        work.pop(0)()
    mc = [[split(v) for v in pair] for pair in m]
    m2 = [[dot_split(v, v) for v in pair] for pair in mc]
    mb = [dot_split(mc[i][0], bc[i]) for i in each]
    if work:
        work.pop(0)()
    m2c = [[split(v) for v in pair] for pair in m2]
    m3 = [[dot_split(m2c[i][j], mc[i][j]) for j in both] for i in each]
    m4 = [[dot_split(v, v) for v in pair] for pair in m2c]
    m2b = [dot_split(m2c[i][0], bc[i]) for i in each]
    m3b = [dot_split(m2c[i][0], split(mb[i])) for i in each]
    if work:
        work.pop(0)()
    n = [[0.75 * m2[i][j] - 0.25 * m3[i][j] for j in both] for i in each]
    p = [
        [
            unit - 0.5 * m[i][j] + 0.375 * m2[i][j] - 0.3125 * m3[i][j] + 0.0625 * m4[i][j]
            for j in both
        ]
        for i in each
    ]
    nb = [split(0.75 * m2b[i] - 0.25 * m3b[i]) for i in each]
    nc = [[split(v) for v in pair] for pair in n]
    pc = [[split(v) for v in pair] for pair in p]
    u = [[split(dot_split(v, v)) for v in pair] for pair in nc]
    r = [[split(dot_split(pc[i][j], split(0.375 * unit + 0.125 * n[i][j]))) for j in both] for i in each]
    pb = [dot_split(pc[i][0], bc[i]) for i in each]
    nnb = [split(dot_split(nc[i][0], nb[i])) for i in each]
    if work:
        work.pop(0)()
    out = []
    for i in each:
        gain = [p[i][j] + dot_split(r[i][j], u[i][j]) for j in both]
        out.append((gain[0], pb[i] + dot_split(r[i][0], nnb[i]), gain[1]))
    for step in work:
        step()
    return out


def columns(q):
    upper, edge, lower = q
    return (
        split(jnp.concatenate([upper, -edge.T], 0)), split(jnp.concatenate([edge, lower], 0))
    )


def turned(q):
    upper, edge, lower = q
    return (
        split(jnp.concatenate([upper, -edge], 1)), split(jnp.concatenate([edge.T, lower], 1))
    )


def choose(flag, a, b):
    return tuple(jnp.where(flag, u, v) for u, v in zip(a, b))


def order(flag, pair):
    return choose(flag, pair[1], pair[0]), choose(flag, pair[0], pair[1])


def beside(a, b, axis=1):
    return tuple(jnp.concatenate([u, v], axis) for u, v in zip(a, b))


def plan(meta_ref):
    flags, signs, kept = [], [], [1.0, 1.0]
    labels = [[meta_ref[p, 0:1, :BW], meta_ref[p, 0:1, BW:]] for p in range(2)]
    names = []
    for r in range(ROUNDS - 1):
        first = [1.0 - meta_ref[p, r + 1:r + 2, :BW] for p in range(2)]
        flag = [jnp.abs(first[p] - kept[p]) < 0.5 for p in range(2)]
        kept = [1.0 - first[0], first[1]]
        labels = [
            [jnp.where(flag[p], labels[p][1], labels[p][0]), jnp.where(flag[p], labels[p][0], labels[p][1])]
            for p in range(2)
        ]
        labels = [[labels[0][0], labels[1][1]], [labels[0][1], labels[1][0]]]
        flags.append(flag)
        signs.append([2.0 * k - 1.0 for k in kept])
        names.append(labels)
    return flags, signs, names


def tall(row):
    return jnp.broadcast_to(row, (BW, BW)).T


def weight(pair):
    return 1.0 / (1.0 + jnp.abs(tall(pair[0]) - pair[1]))


def begin(p, diag, meta_ref, turn_ref, flip_ref, diag_ref, work=()):
    unit = eye(BW)
    labels = meta_ref[p, 0:1, :]
    left = jnp.sum(diag[:BW, :BW] * unit, axis=1, keepdims=True)
    right = jnp.sum(diag[BW:, BW:] * unit, axis=0, keepdims=True)
    scale = lax.rsqrt(left + epsilon) * lax.rsqrt(right + epsilon)
    cross = diag[:BW, BW:] * (scale * weight((labels[:, :BW], labels[:, BW:])))
    (q,) = rotate([cross], [1.0], work)
    flag = meta_ref[p, 1:2, :BW] < 0.5
    q_cut = beside(*order(flag, columns(q)))
    wide = jnp.concatenate([flag, flag], 1)
    flip = beside(*order(wide, turned(q)), 0)
    for k in range(2):
        turn_ref[p, k] = q_cut[k]
        flip_ref[p, k] = flip[k]
    diag_ref[p] = fine_right(flip, cut3(fine_left(cut3(diag), q_cut)))


def prepare(pos, meta_ref, diag_ref, fac_ref):
    unit = eye(BW)
    flags, signs, names = plan(meta_ref)

    def scales(p, s, axis):
        part = slice(s * BW, s * BW + BW)
        return lax.rsqrt(jnp.sum(diag_ref[p, part, part] * unit, axis=axis, keepdims=True) + epsilon)

    fac_ref[0] = weight(names[0][0]) * scales(0, 0, 1) * scales(1, 1, 0)
    fac_ref[1] = weight(names[0][1]) * scales(0, 1, 1) * scales(1, 0, 0)
    fac_ref[2] = weight(names[1][0])
    fac_ref[3] = weight(names[1][1])
    fac_ref[4] = weight([jnp.where(pos == 0, a, b) for a, b in zip(*names[2])])


def chain(pos, between, diag_ref, turn_ref, flip_ref, meta_ref, fac_ref, high_ref, low_ref):
    assert ROUNDS == 4
    flags, signs, _ = plan(meta_ref)
    low, top = slice(0, BW), slice(BW, 2 * BW)
    turn = [(turn_ref[p, 0], turn_ref[p, 1]) for p in range(2)]

    def part(pair, rows=slice(None), cols=slice(None)):
        return tuple(v[rows, cols] for v in pair)

    held = {}
    x0, x1 = between[low, top], between[top, low]
    held["stay"], held["move"] = between[low, low], between[top, top]
    qs = rotate([x0 * fac_ref[0], x1 * fac_ref[1]], signs[0])
    d0 = jnp.concatenate([
        jnp.concatenate([diag_ref[0, low, low], x0], 1),
        jnp.concatenate([x0.T, diag_ref[1, top, top]], 1),
    ], 0)
    d1 = jnp.concatenate([
        jnp.concatenate([diag_ref[0, top, top], x1], 1),
        jnp.concatenate([x1.T, diag_ref[1, low, low]], 1),
    ], 0)
    g = jnp.concatenate([
        jnp.concatenate([diag_ref[0, low, top], held["stay"]], 1),
        jnp.concatenate([held["move"].T, diag_ref[1, top, low]], 1),
    ], 0)
    small = eye(2 * BW)
    row0 = jnp.sum(d0 * small, axis=0, keepdims=True)
    tall1 = jnp.sum(d1 * small, axis=1, keepdims=True)
    d0, d1, g = split(d0 - row0 * small), split(d1 - tall1 * small), split(g)
    q = [beside(*order(flags[1][p], columns(qs[p]))) for p in range(2)]
    wide = [jnp.concatenate([flags[1][p]] * 2, 1) for p in range(2)]
    qt = [beside(*order(wide[p], turned(qs[p])), 0) for p in range(2)]

    def full(pair):
        return pair[0].astype(jnp.float32) + pair[1].astype(jnp.float32)

    mid = split(dot_split(g, q[1]))
    t0 = full(qt[0]) * row0 + dot_split(qt[0], d0)
    t1 = full(q[1]) * tall1 + dot_split(d1, q[1])
    x0 = dot_split(part(qt[0], low), part(mid, cols=top))
    x1 = dot_split(part(qt[0], top), part(mid, cols=low))

    sq0 = lax.rsqrt(jnp.sum(full(qt[0]) * t0, axis=1, keepdims=True) + epsilon)
    sq1 = lax.rsqrt(jnp.sum(full(q[1]) * t1, axis=0, keepdims=True) + epsilon)

    def rest0():
        held["stay"] = dot_split(part(qt[0], low), part(mid, cols=low))
        held["move"] = dot_split(part(qt[0], top), part(mid, cols=top))
        held["d0"] = fine_left(cut3(t0), q[0])

    def rest1():
        held["d1"] = fine_right(qt[1], cut3(t1))
        held["w00"] = dot_split(part(turn[0], cols=low), part(q[0], low))

    def rest2():
        held["w01"] = dot_split(part(turn[1], cols=top), part(q[0], top))
        held["w10"] = dot_split(part(turn[0], cols=top), part(q[1], low))

    def rest3():
        held["w11"] = dot_split(part(turn[1], cols=low), part(q[1], top))

    qs = rotate(
        [x0 * (fac_ref[2] * sq0[low] * sq1[:, top]), x1 * (fac_ref[3] * sq0[top] * sq1[:, low])],
        signs[1], [rest0, rest1, rest2, rest3],
    )
    e0, e1 = held["d0"], held["d1"]
    d0 = split(jnp.concatenate([
        jnp.concatenate([e0[low, low], x0], 1), jnp.concatenate([x0.T, e1[top, top]], 1),
    ], 0))
    d1 = split(jnp.concatenate([
        jnp.concatenate([e0[top, top], x1], 1), jnp.concatenate([x1.T, e1[low, low]], 1),
    ], 0))
    g = split(jnp.concatenate([
        jnp.concatenate([e0[low, top], held["stay"]], 1),
        jnp.concatenate([held["move"].T, e1[top, low]], 1),
    ], 0))
    mine = pos == 0
    wide = jnp.concatenate([flags[2][0]] * 2, 1)
    stay, move = order(wide, turned(qs[0]))
    up = choose(mine, stay, move)
    stay, move = order(flags[2][0], columns(qs[0]))
    upright = choose(mine, stay, move)
    stay, move = order(flags[2][1], columns(qs[1]))
    side = choose(mine, move, stay)
    mid = split(dot_split(g, side))
    t0 = dot_split(up, d0)
    t1 = dot_split(d1, side)
    x = dot_split(up, mid)
    sq0 = lax.rsqrt(jnp.sum(full(up) * t0, axis=1, keepdims=True) + epsilon)
    sq1 = lax.rsqrt(jnp.sum(full(side) * t1, axis=0, keepdims=True) + epsilon)
    rows = [None, None]

    def tail(r):
        def run():
            a, b = held["w0" + str(r)], held["w1" + str(r)]
            first = split(jnp.concatenate([a[:, low], b[:, top]], 1))
            second = split(jnp.concatenate([a[:, top], b[:, low]], 1))
            rows[r] = split(jnp.concatenate([dot_split(first, upright), dot_split(second, side)], 1))
        return run

    sign = jnp.where(mine, signs[2][0], signs[2][1])
    (last,) = rotate([x * (fac_ref[4] * sq0 * sq1)], [sign], [tail(0), tail(1)])
    a, b = columns(last)
    last = beside(choose(sign > 0.0, a, b), choose(sign > 0.0, b, a))
    out = [split(dot_split(rows[r], last)) for r in range(2)]
    width = 2 * BW
    for p in range(2):
        high, lower = choose(mine, out[p], out[1 - p])
        high_ref[p * width:(p + 1) * width] = high
        low_ref[p * width:(p + 1) * width] = lower


def write_kernel(tile, held_ref, high_ref, low_ref, last_high, last_low, out_ref, made, sems):
    early, rows = held_ref.shape[0], out_ref.shape[0]
    pos = lax.axis_index("blk")
    copies = []

    def write(t, source):
        there = pl.ds(pl.multiple_of(lax.rem(pos * (rows // 2) + t * tile, rows), tile), tile)
        copies.append(pltpu.make_async_copy(source, out_ref.at[there], sems.at[t]))
        copies[-1].start()

    for t in range(early // tile):
        write(t, held_ref.at[pl.ds(t * tile, tile)])
    for t in range(early // tile, rows // tile):
        here = slice(t * tile - early, (t + 1) * tile - early)
        made[here, :] = dot_split((last_high[here, :], last_low[here, :]), (high_ref[...], low_ref[...]))
        write(t, made.at[pl.ds(t * tile - early, tile)])
    for copy in copies:
        copy.wait()


def pair_body(n, snapshots, grades, mover):
    rows, width = snapshots.shape
    share = width // n
    f32 = jnp.float32
    dma = pltpu.SemaphoreType.DMA
    whole = pltpu.VMEM((2, n // 2, share, width), f32)
    part = pltpu.VMEM((n // 2, share, width), f32)
    one = pltpu.VMEM((share, width), f32)
    everything = pltpu.VMEM((rows, width), f32)
    cut = pltpu.VMEM((rows, width), jnp.bfloat16)
    square = pltpu.VMEM((2, width, width), f32)
    turn = pltpu.VMEM((2, 2, width, width), jnp.bfloat16)
    operands = [
        pltpu.with_memory_space_constraint(value, pltpu.HBM)
        for value in (snapshots, grades.reshape(1, width), mover.reshape(ROUNDS - 1))
    ]
    tile = TALL * (rows // 2 // CHUNKS)
    late = rows // 2
    bf16 = jnp.bfloat16
    made = pl.pallas_call(
        functools.partial(turn_kernel, n),
        out_shape=(
            jax.ShapeDtypeStruct((rows - late, width), f32),
            jax.ShapeDtypeStruct((2 * width, width), bf16),
            jax.ShapeDtypeStruct((2 * width, width), bf16),
            jax.ShapeDtypeStruct((late, 2 * width), bf16),
            jax.ShapeDtypeStruct((late, 2 * width), bf16),
        ),
        in_specs=[HBM] * 3,
        out_specs=(VMEM,) * 5,
        scratch_shapes=[
            everything, everything, cut, cut, cut, cut, pltpu.VMEM((1, width), jnp.int32),
            pltpu.SMEM((ROUNDS - 1,), jnp.int32),
            pltpu.VMEM((2, 8, width), f32), pltpu.VMEM((8, width), f32),
            whole, part, part, part, pltpu.VMEM((2, 2, n // 2, share, width), f32), square, turn, turn,
            pltpu.VMEM((5, BW, BW), f32),
            whole, part, part, part, one, one, whole,
            dma((2 * CHUNKS,)), dma((2 * CHUNKS,)),
            dma((2, n // 2)), dma((2, n // 2)), dma((3, n // 2)), dma((3, n // 2)),
            dma((4,)), dma((4,)), dma((3,)), dma((3,)), dma((n // 2,)), dma((n // 2,)),
            dma((LOADS,)), dma((2,)), pltpu.SemaphoreType.REGULAR,
        ],
        compiler_params=pltpu.CompilerParams(
            collective_id=0, has_side_effects=True, vmem_limit_bytes=40 * 1024 * 1024
        ),
    )(*operands)
    return pl.pallas_call(
        functools.partial(write_kernel, tile),
        out_shape=jax.ShapeDtypeStruct((rows, width), f32),
        in_specs=[VMEM] * 5,
        out_specs=ANY,
        scratch_shapes=[pltpu.VMEM((late, width), f32), dma((rows // tile,))],
        compiler_params=pltpu.CompilerParams(vmem_limit_bytes=8 * 1024 * 1024),
    )(*made)


def solution(mesh):
    placed = (P("rows", "blk"), P("blk"), P(None, "blk"))
    n = mesh.shape["rows"]
    pairs = mesh.shape["blk"] == 2 and n % 2 == 0 and (2 * BW) % (8 * n) == 0
    body = functools.partial(pair_body, n) if pairs else general_body
    return jax.shard_map(
        body, mesh=mesh, in_specs=placed, out_specs=P("rows", "blk"), check_vma=False
    )
```
